32 devices in a mesh: expert: 16 (over z, y, x), fsdp: 2 (over core).
Axes of the slice: x: 2, y: 2, z: 4, core: 2. Of those that a mesh axis runs over, the one named last changes fastest.
Arguments:
- tokens: bfloat16 [4096, 512], P(('expert', 'fsdp')), may hold values from -6 to 6
- out_grad: bfloat16 [4096, 512], P(('expert', 'fsdp')), may hold values from -6 to 6
- gates: bfloat16 [4096, 2], P('expert'), may hold values from 0.099609375 to 1
- expert_ids: int32 [4096, 2], P('expert'), may hold values from 0 to 15, as said below
- w_in: bfloat16 [16, 512, 4096], P('expert', None, 'fsdp'), may hold values from -0.25 to 0.25
- w_out: bfloat16 [16, 512, 4096], P('expert', None, 'fsdp'), may hold values from -0.09375 to 0.09375
Outputs:
- d_tokens: bfloat16 [4096, 512], P(('expert', 'fsdp'))
- d_gates: float32 [4096, 2], P(('expert', 'fsdp'))
- d_w_in: bfloat16 [16, 512, 4096], P('expert', None, 'fsdp')
- d_w_out: bfloat16 [16, 512, 4096], P('expert', None, 'fsdp')
The draws below stay inside these ranges and needn't reach their ends.
Inputs may be any that keep to these rules, and one draw needn't show every extreme that they name: `expert_ids`: each token names two different experts. Within each aligned block of 128 tokens (the tokens of one device) no expert is named more than 20 times, and in every block some expert is named exactly 20 times.
All inputs are finite; a program needn't handle non-finite values.
Results may differ from the reference program's by a relative error of at most 0.011.
Values may be sent and summed in bfloat16 or wider, within the bound.
No kernel may reach another device: no remote copies, remote signals or barrier semaphores. Data moves between devices by JAX's collectives and lax.ppermute only.
A program may use at most 64 MiB of HBM per device.

```python
import jax
import jax.numpy as jnp
from jax import lax

D = 512
F = 4096
TOK_DEV = 128
EXPERTS = 16
CAP = 20
TOKENS = 4096
N_FSDP = 2


def one_block(block_key):
    keys = jax.random.split(block_key, 5)
    pull = jax.random.randint(keys[0], (EXPERTS,), 1, 9)
    noise = jax.random.randint(keys[1], (EXPERTS, CAP), 0, 1024)
    column = jnp.arange(CAP, dtype=jnp.int32)[None, :]
    score = column * pull[:, None] * 1024 + noise
    forced = jax.random.randint(keys[2], (), 0, EXPERTS)
    chosen = jnp.arange(EXPERTS, dtype=jnp.int32)[:, None] == forced
    score = jnp.where(chosen, column - 1048576, score)
    flat = score.reshape(-1) * 512 + jnp.arange(EXPERTS * CAP, dtype=jnp.int32)
    picked = jnp.sort(jnp.argsort(flat, stable=True)[:2 * TOK_DEV])
    owners = (picked // CAP).astype(jnp.int32)
    order = jax.random.permutation(keys[3], TOK_DEV)
    first = owners[:TOK_DEV][order]
    second = owners[TOK_DEV:][order]
    flip = jax.random.randint(keys[4], (TOK_DEV,), 0, 2) == 1
    return jnp.stack([jnp.where(flip, second, first), jnp.where(flip, first, second)], axis=1)


def route_blocks(key):
    blocks = TOKENS // TOK_DEV
    keys = jax.random.split(jax.random.fold_in(key, 31), blocks)
    return jax.vmap(one_block)(keys).reshape(TOKENS, 2).astype(jnp.int32)


def draw_expert_ids(key, part):
    return route_blocks(key)


def shard_levels(key, dims, cuts, least, largest):
    factor_of, own = 1.0, jax.random.fold_in(key, 6)
    for axis_at, shards_of in cuts:
        heights = jnp.exp(jax.random.uniform(jax.random.fold_in(own, axis_at), (shards_of,), jnp.float32, least / len(cuts), largest / len(cuts)))
        factor_of = factor_of * jnp.repeat(heights, dims[axis_at] // shards_of).reshape([-1 if axis == axis_at else 1 for axis in range(len(dims))])
    return factor_of


def normal_values(stream_key, shape, deviation, most, cuts=(), kind=jnp.bfloat16):
    loudness = shard_levels(stream_key, shape, cuts, -0.22, 0.18) if cuts else 1.0
    drawn = jax.random.normal(stream_key, shape, jnp.float32) * deviation * loudness
    return jnp.minimum(jnp.maximum(drawn, -most), most).astype(kind)


def setup_inputs(seed: int = 0) -> dict:
    key_list = jax.random.split(jax.random.key(seed), 7)
    return {
        "tokens": normal_values(key_list[0], (TOKENS, D), 1.0, 6.0, ((0, 32),)),
        "out_grad": normal_values(key_list[1], (TOKENS, D), 0.5, 6.0, ((0, 32),)),
        "gates": jnp.clip(0.099609375 + 0.9003906 * jax.random.uniform(key_list[2], (TOKENS, 2), jnp.float32) ** shard_levels(key_list[2], (TOKENS, 2), ((0, 16),), -0.2, 0.2), 0.099609375, 1.0).astype(jnp.bfloat16),
        "expert_ids": draw_expert_ids(jax.random.fold_in(key_list[6], 71), 0),
        "w_in": normal_values(key_list[4], (EXPERTS, D, F), D ** -0.5, 0.25, ((0, 16), (2, 2))),
        "w_out": normal_values(key_list[5], (EXPERTS, D, F), F ** -0.5, 0.09375, ((0, 16), (2, 2))),
    }


COEF = 0.7978845608
CUBIC = 0.044715


def gelu_parts(pre_act):
    inner = COEF * (pre_act + CUBIC * pre_act * pre_act * pre_act)
    tangent = jnp.tanh(inner)
    values = 0.5 * pre_act * (1.0 + tangent)
    slopes = 0.5 * (1.0 + tangent) + 0.5 * pre_act * (1.0 - tangent * tangent) * COEF * (1.0 + 3.0 * CUBIC * pre_act * pre_act)
    return values, slopes


def slot_ranks(route_ids):
    count = route_ids.shape[1]
    same = route_ids[:, :, None] == route_ids[:, None, :]
    earlier = jnp.arange(count)[None, :] < jnp.arange(count)[:, None]
    return jnp.sum(jnp.logical_and(same, earlier[None]), axis=2).astype(jnp.int32)


def reference(tokens, out_grad, gates, expert_ids, w_in, w_out):
    blocks = TOKENS // TOK_DEV
    per_block = 2 * TOK_DEV
    span = F // N_FSDP
    block_ids = expert_ids.reshape(blocks, per_block).astype(jnp.int32)
    ranks = slot_ranks(block_ids)
    assign = jnp.arange(TOKENS * 2, dtype=jnp.int32).reshape(blocks, per_block)
    block_index = jnp.broadcast_to(jnp.arange(blocks, dtype=jnp.int32)[:, None], (blocks, per_block))
    table = jnp.full((EXPERTS, blocks, CAP), -1, jnp.int32).at[block_ids, block_index, ranks].set(assign)
    table = table.reshape(EXPERTS, blocks * CAP)
    gate_flat = gates.reshape(-1).astype(jnp.float32)

    def per_expert(carry, inputs):
        token_acc, gate_acc = carry
        rows, in_mat, out_mat = inputs
        valid = rows >= 0
        safe = jnp.where(valid, rows, 0).astype(jnp.int32)
        token_row = safe // 2
        x_rows = tokens[token_row]
        dy_rows = out_grad[token_row]
        scale = jnp.where(valid, gate_flat[safe], jnp.float32(0.0))[:, None]
        pre_act = jnp.dot(x_rows, in_mat, preferred_element_type=jnp.float32)
        grad_act = jnp.dot(dy_rows, out_mat, preferred_element_type=jnp.float32)
        values, slopes = gelu_parts(pre_act)
        act_scaled = (scale * values).astype(jnp.bfloat16)
        grad_pre = (scale * grad_act * slopes).astype(jnp.bfloat16)
        grad_out = jnp.dot(dy_rows.T, act_scaled, preferred_element_type=jnp.float32).astype(jnp.bfloat16)
        grad_in = jnp.dot(x_rows.T, grad_pre, preferred_element_type=jnp.float32).astype(jnp.bfloat16)
        count = rows.shape[0]
        token_part = jnp.einsum("rbk,dbk->brd", grad_pre.astype(jnp.float32).reshape(count, N_FSDP, span), in_mat.astype(jnp.float32).reshape(D, N_FSDP, span)).astype(jnp.bfloat16)
        token_slot = jnp.sum(token_part.astype(jnp.float32), axis=0)
        gate_part = jnp.sum((grad_act * values).reshape(count, N_FSDP, span), axis=2).astype(jnp.bfloat16)
        gate_slot = jnp.sum(gate_part.astype(jnp.float32), axis=1)
        token_acc = token_acc.at[token_row].add(jnp.where(valid[:, None], token_slot, jnp.float32(0.0)))
        gate_acc = gate_acc.at[safe].add(jnp.where(valid, gate_slot, jnp.float32(0.0)))
        return (token_acc, gate_acc), (grad_in, grad_out)

    init = (jnp.zeros((TOKENS, D), jnp.float32), jnp.zeros((TOKENS * 2,), jnp.float32))
    (token_acc, gate_acc), (d_w_in, d_w_out) = lax.scan(per_expert, init, (table, w_in, w_out))
    return token_acc.astype(jnp.bfloat16), gate_acc.reshape(TOKENS, 2), d_w_in, d_w_out
```

```python
import functools

import jax
import jax.numpy as jnp
from jax import lax
from jax.experimental import pallas as pl
from jax.experimental.pallas import tpu as pltpu
from jax.sharding import PartitionSpec as P

COEF = 0.7978845608
CUBIC = 0.044715
ROW_DIMS = (((0,), (0,)), ((), ()))
LAST_DIMS = (((1,), (1,)), ((), ()))
LANES = 128
TILE = 8
PACK = 16
MIB = 1 << 20


def gelu_parts(pre_act):
    square = pre_act * pre_act
    half = 0.5 + 0.5 * jnp.tanh(pre_act * (COEF + (COEF * CUBIC) * square))
    values = pre_act * half
    slopes = half + values * ((1.0 - half) * (2.0 * COEF + (6.0 * COEF * CUBIC) * square))
    return values, slopes


def iota(shape, dim):
    return lax.broadcasted_iota(jnp.int32, shape, dim)


def one_hot(mask):
    return jnp.where(mask, 1.0, 0.0).astype(jnp.bfloat16)


class Plan:
    def __init__(self, experts, groups, tok_dev, width):
        self.experts, self.groups, self.tok_dev, self.width = experts, groups, tok_dev, width
        self.cap = 5 * tok_dev // (2 * experts)
        self.main = self.cap // PACK * PACK
        self.tail = self.cap - self.main
        self.send = 2 * self.cap
        self.back = self.main + TILE
        self.slots = experts * self.cap
        self.heads = experts * self.main

    def fits(self):
        return (
            self.groups == 2
            and self.main > 0
            and 2 * self.tail == TILE
            and self.cap <= LANES
            and self.tok_dev % LANES == 0
            and self.width % LANES == 0
        )


def dispatch_kernel(plan, ids_ref, gates_ref, x_ref, dy_ref, send_ref, route_ref):
    tokens = plan.tok_dev
    mine = pl.ds(pl.multiple_of(lax.axis_index("fsdp") * tokens, LANES), tokens)
    ids = ids_ref[:, mine]
    gates = gates_ref[:, mine].astype(jnp.float32)
    expert = iota((plan.experts, tokens), 0)
    named = [expert == ids[k : k + 1, :] for k in range(2)]
    earlier = one_hot(iota((tokens, tokens), 0) < iota((tokens, tokens), 1))
    counts = jnp.dot(one_hot(named[0] | named[1]), earlier, preferred_element_type=jnp.float32)
    row = iota((plan.experts * plan.send, tokens), 0)
    x_pick, dy_pick = False, 0.0
    for k in range(2):
        rank = jnp.sum(jnp.where(named[k], counts, 0.0), axis=0, keepdims=True).astype(jnp.int32)
        first = ids[k : k + 1, :] * plan.send + rank
        head = rank < plan.main
        x_pick = x_pick | (row == first + jnp.where(head, 0, plan.main))
        dy_pick = dy_pick + jnp.where(
            row == first + jnp.where(head, plan.main, plan.cap), gates[k : k + 1, :], 0.0
        )
        route_ref[k : k + 1, :] = ids[k : k + 1, :]
        route_ref[2 + k : 3 + k, :] = rank
        route_ref[4 + k : 5 + k, :] = jnp.zeros_like(rank)
        route_ref[6 + k : 7 + k, :] = jnp.zeros_like(rank)
    send = jnp.dot(one_hot(x_pick), x_ref[...], preferred_element_type=jnp.float32)
    send = send + jnp.dot(
        dy_pick.astype(jnp.bfloat16), dy_ref[...], preferred_element_type=jnp.float32
    )
    send_ref[...] = send.astype(jnp.bfloat16)


def unpack(plan, recv_ref, x_all, dy_all, at):
    main, tail, width = plan.main, plan.tail, plan.width
    tails = plan.experts * tail
    heads = pl.ds(at, plan.heads)
    x_all[heads, :] = recv_ref[:, :main, :].reshape(plan.heads, width)
    dy_all[heads, :] = recv_ref[:, main : 2 * main, :].reshape(plan.heads, width)
    mixed = recv_ref[:, 2 * main :, :].reshape(plan.experts * TILE, width)
    place, source = iota((2 * tails, plan.experts * TILE), 0), iota(
        (2 * tails, plan.experts * TILE), 1
    )
    second = jnp.where(place >= tails, 1, 0)
    slot = place - second * tails
    pick = one_hot(source == slot // tail * TILE + slot % tail + second * tail)
    split = jnp.dot(pick, mixed, preferred_element_type=jnp.float32).astype(jnp.bfloat16)
    x_all[pl.ds(at + plan.heads, tails), :] = split[:tails]
    dy_all[pl.ds(at + plan.heads, tails), :] = split[tails:]


def token_kernel(
    plan, steps, recv_ref, in_a, out_a, in_b, out_b, back_ref, x_all, dy_all, total, gate_total
):
    step = pl.program_id(0)

    @pl.when(step == 0)
    def _():
        unpack(plan, recv_ref, x_all, dy_all, 0)
        total[...] = jnp.zeros_like(total)
        gate_total[...] = jnp.zeros_like(gate_total)

    def work(in_ref, out_ref):
        in_mat = in_ref[...]
        pre_act = jnp.dot(x_all[...], in_mat, preferred_element_type=jnp.float32)
        grad_act = jnp.dot(dy_all[...], out_ref[...], preferred_element_type=jnp.float32)
        values, slopes = gelu_parts(pre_act)
        grad_pre = (grad_act * slopes).astype(jnp.bfloat16)
        total[...] += lax.dot_general(
            grad_pre, in_mat, LAST_DIMS, preferred_element_type=jnp.float32
        )
        product = grad_act * values
        part = product[:, :LANES]
        for at in range(LANES, product.shape[1], LANES):
            part = part + product[:, at : at + LANES]
        gate_total[...] += part

    @pl.when(step < steps)
    def _():
        work(in_a, out_a)

    @pl.when(step >= steps)
    def _():
        work(in_b, out_b)

    @pl.when(step == 2 * steps - 1)
    def _():
        main, tail, width = plan.main, plan.tail, plan.width
        tails = plan.experts * tail
        part = total[...].astype(jnp.bfloat16)
        back_ref[:, :main, :] = part[: plan.heads].reshape(plan.experts, main, width)
        gate = jnp.sum(gate_total[...], axis=1, keepdims=True)
        slot = iota((plan.slots, LANES), 0)
        over = slot - plan.heads
        rank = jnp.where(over >= 0, main + over % tail, slot % main)
        gate_rows = jnp.where(iota((plan.slots, LANES), 1) == rank, gate, 0.0).astype(jnp.bfloat16)
        place, slot = iota((plan.experts * TILE, plan.slots), 0), iota(
            (plan.experts * TILE, plan.slots), 1
        )
        over = slot - plan.heads
        source = jnp.where(over >= 0, over // tail, slot // main)
        gates = jnp.dot(
            one_hot(place == source * TILE + tail), gate_rows, preferred_element_type=jnp.float32
        )
        place, slot = iota((plan.experts * TILE, tails), 0), iota((plan.experts * TILE, tails), 1)
        rest = jnp.dot(
            one_hot(place == slot // tail * TILE + slot % tail),
            part[plan.heads :],
            preferred_element_type=jnp.float32,
        )
        rest = jnp.concatenate([rest[:, :LANES] + gates, rest[:, LANES:]], axis=1)
        back_ref[:, main:, :] = rest.astype(jnp.bfloat16).reshape(plan.experts, TILE, width)


def weight_kernel(plan, own_ref, other_ref, in_ref, out_ref, grad_in_ref, grad_out_ref, x_all, dy_all):
    @pl.when(pl.program_id(0) == 0)
    def _():
        unpack(plan, own_ref, x_all, dy_all, 0)
        unpack(plan, other_ref, x_all, dy_all, plan.slots)

    x_rows, dy_rows = x_all[...], dy_all[...]
    pre_act = jnp.dot(x_rows, in_ref[...], preferred_element_type=jnp.float32)
    grad_act = jnp.dot(dy_rows, out_ref[...], preferred_element_type=jnp.float32)
    values, slopes = gelu_parts(pre_act)
    grad_pre = (grad_act * slopes).astype(jnp.bfloat16)
    grad_in_ref[...] = lax.dot_general(
        x_rows, grad_pre, ROW_DIMS, preferred_element_type=jnp.float32
    ).astype(jnp.bfloat16)
    grad_out_ref[...] = lax.dot_general(
        dy_rows, values.astype(jnp.bfloat16), ROW_DIMS, preferred_element_type=jnp.float32
    ).astype(jnp.bfloat16)


def combine_kernel(plan, route_ref, gates_ref, back_ref, token_ref, gate_ref):
    tokens, rows = plan.tok_dev, plan.experts * plan.back
    mine = pl.ds(pl.multiple_of(lax.axis_index("fsdp") * tokens, LANES), tokens)
    gates = gates_ref[:, mine].astype(jnp.float32)
    back = back_ref[...]
    row = iota((rows, tokens), 0)
    pick = False
    for k in range(2):
        pick = pick | (row == route_ref[k : k + 1, :] * plan.back + route_ref[2 + k : 3 + k, :])
    token_ref[...] = lax.dot_general(
        one_hot(pick), back, ROW_DIMS, preferred_element_type=jnp.float32
    ).astype(jnp.bfloat16)
    gate_row = iota((plan.experts, rows), 0) * plan.back + plan.cap
    gate_rows = jnp.dot(
        one_hot(iota((plan.experts, rows), 1) == gate_row),
        back[:, :LANES],
        preferred_element_type=jnp.float32,
    ).astype(jnp.bfloat16)
    for k in range(2):
        named = one_hot(iota((plan.experts, tokens), 0) == route_ref[k : k + 1, :])
        slots = lax.dot_general(gate_rows, named, ROW_DIMS, preferred_element_type=jnp.float32)
        here = iota((LANES, tokens), 0) == route_ref[2 + k : 3 + k, :]
        total = jnp.sum(jnp.where(here, slots, 0.0), axis=0, keepdims=True)
        gate_ref[k : k + 1, :] = total / gates[k : k + 1, :]


def params(mib):
    return pltpu.CompilerParams(vmem_limit_bytes=mib * MIB)


def whole(shape):
    return pl.BlockSpec(shape, lambda *_: (0,) * len(shape))


def moved_rows(plan, tokens, out_grad, gates, expert_ids, w_in, w_out):
    experts, width, slots = plan.experts, plan.width, plan.slots
    in_own, out_own = w_in[0], w_out[0]
    hidden = in_own.shape[1]
    swap = [(0, 1), (1, 0)]
    in_other = lax.ppermute(in_own, "fsdp", swap)
    out_other = lax.ppermute(out_own, "fsdp", swap)
    ids, gate_rows = expert_ids.T, gates.T
    bf16, f32 = jnp.bfloat16, jnp.float32

    send, route = pl.pallas_call(
        functools.partial(dispatch_kernel, plan),
        out_shape=(
            jax.ShapeDtypeStruct((experts * plan.send, width), bf16),
            jax.ShapeDtypeStruct((TILE, plan.tok_dev), jnp.int32),
        ),
        compiler_params=params(16),
        name="dispatch",
    )(ids, gate_rows, tokens, out_grad)
    recv = lax.all_to_all(
        send.reshape(experts, plan.send, width), "expert", split_axis=0, concat_axis=0, tiled=True
    )
    recv_other = lax.ppermute(recv, "fsdp", swap)

    block = min(512, hidden)
    steps = hidden // block
    own_spec = pl.BlockSpec((width, block), lambda i: (0, jnp.minimum(i, steps - 1)))
    other_spec = pl.BlockSpec((width, block), lambda i: (0, jnp.maximum(i - steps, 0)))
    back = pl.pallas_call(
        functools.partial(token_kernel, plan, steps),
        grid=(2 * steps,),
        in_specs=[whole(recv.shape), own_spec, own_spec, other_spec, other_spec],
        out_specs=whole((experts, plan.back, width)),
        out_shape=jax.ShapeDtypeStruct((experts, plan.back, width), bf16),
        scratch_shapes=[
            pltpu.VMEM((slots, width), bf16),
            pltpu.VMEM((slots, width), bf16),
            pltpu.VMEM((slots, width), f32),
            pltpu.VMEM((slots, LANES), f32),
        ],
        cost_estimate=pl.CostEstimate(
            flops=12 * slots * width * hidden,
            transcendentals=2 * slots * hidden,
            bytes_accessed=8 * width * hidden,
        ),
        compiler_params=params(24),
        name="token_grad",
    )(recv, in_own, out_own, in_other, out_other)
    returned = lax.all_to_all(back, "expert", split_axis=0, concat_axis=0, tiled=True)

    spec = pl.BlockSpec((width, block), lambda i: (0, i))
    grad_in, grad_out = pl.pallas_call(
        functools.partial(weight_kernel, plan),
        grid=(steps,),
        in_specs=[whole(recv.shape), whole(recv.shape), spec, spec],
        out_specs=(spec, spec),
        out_shape=(jax.ShapeDtypeStruct((width, hidden), bf16),) * 2,
        scratch_shapes=[pltpu.VMEM((2 * slots, width), bf16), pltpu.VMEM((2 * slots, width), bf16)],
        cost_estimate=pl.CostEstimate(
            flops=16 * slots * width * hidden,
            transcendentals=2 * slots * hidden,
            bytes_accessed=8 * width * hidden,
        ),
        compiler_params=params(24),
        name="weight_grad",
    )(recv, recv_other, in_own, out_own)

    d_tokens, d_gates = pl.pallas_call(
        functools.partial(combine_kernel, plan),
        out_shape=(
            jax.ShapeDtypeStruct((plan.tok_dev, width), bf16),
            jax.ShapeDtypeStruct((2, plan.tok_dev), f32),
        ),
        compiler_params=params(16),
        name="combine",
    )(route, gate_rows, returned.reshape(experts * plan.back, width))
    return d_tokens, d_gates.T, grad_in[None], grad_out[None]


def slot_ranks(route_ids):
    count = route_ids.shape[1]
    same = route_ids[:, :, None] == route_ids[:, None, :]
    earlier = jnp.arange(count)[None, :] < jnp.arange(count)[:, None]
    return jnp.sum(jnp.logical_and(same, earlier[None]), axis=2)


def fill_slots(owner, rows_x, rows_dy, gate_flat):
    valid = owner >= 0
    safe = jnp.where(valid, owner, 0)
    token_row = safe // 2
    x_buf = jnp.where(valid[:, None], rows_x[token_row], jnp.zeros((), rows_x.dtype))
    dy_buf = jnp.where(valid[:, None], rows_dy[token_row], jnp.zeros((), rows_dy.dtype))
    gate_buf = jnp.where(valid, gate_flat[safe], jnp.zeros((), gate_flat.dtype))
    return (x_buf, dy_buf, gate_buf)


def expert_work(x_rows, dy_rows, gate_rows, in_shard, out_shard):
    pre_act = jnp.dot(x_rows, in_shard, preferred_element_type=jnp.float32)
    grad_act = jnp.dot(dy_rows, out_shard, preferred_element_type=jnp.float32)
    values, slopes = gelu_parts(pre_act)
    scale = gate_rows.astype(jnp.float32)[:, None]
    act_scaled = (scale * values).astype(jnp.bfloat16)
    grad_pre = (scale * grad_act * slopes).astype(jnp.bfloat16)
    grad_out = lax.dot_general(dy_rows, act_scaled, ROW_DIMS, preferred_element_type=jnp.float32)
    grad_in = lax.dot_general(x_rows, grad_pre, ROW_DIMS, preferred_element_type=jnp.float32)
    token_part = lax.dot_general(
        grad_pre, in_shard, LAST_DIMS, preferred_element_type=jnp.float32
    ).astype(jnp.bfloat16)
    gate_part = jnp.sum(grad_act * values, axis=1).astype(jnp.bfloat16)
    return (grad_in, grad_out, token_part, gate_part)


def all_rows(plan, tokens, out_grad, gates, expert_ids, w_in, w_out):
    tok_dev, width, groups = plan.tok_dev, plan.width, plan.groups
    experts, capacity = plan.experts, plan.cap
    group_ids = expert_ids.reshape(groups, 2 * tok_dev)
    group_gates = gates.reshape(groups, 2 * tok_dev)
    group_ranks = slot_ranks(group_ids)
    all_x = lax.all_gather(tokens, "fsdp", axis=0, tiled=True)
    all_dy = lax.all_gather(out_grad, "fsdp", axis=0, tiled=True)
    member = jnp.arange(groups, dtype=jnp.int32)[:, None]
    target = ((group_ids * groups + member) * capacity + group_ranks).reshape(-1)
    owner = (
        jnp.full((experts * groups * capacity,), -1, jnp.int32)
        .at[target]
        .set(jnp.arange(2 * tok_dev * groups, dtype=jnp.int32))
    )
    span = groups * capacity
    total_rows = experts * span

    def exchange(rows):
        rows = rows.reshape((experts, span) + rows.shape[1:])
        rows = lax.all_to_all(rows, "expert", split_axis=0, concat_axis=0, tiled=True)
        return rows.reshape((total_rows,) + rows.shape[2:])

    buffers = fill_slots(owner, all_x, all_dy, group_gates.reshape(-1))
    grad_in, grad_out, token_part, gate_part = expert_work(
        *(exchange(b) for b in buffers), w_in[0], w_out[0]
    )
    token_back, gate_back = exchange(token_part), exchange(gate_part)
    token_pick = token_back[target].astype(jnp.float32).reshape(groups * tok_dev, 2, width)
    gate_terms = gate_back[target].astype(jnp.float32).reshape(groups * tok_dev, 2)

    def spread(terms):
        return lax.psum_scatter(
            terms.astype(jnp.bfloat16), "fsdp", scatter_dimension=0, tiled=True
        )

    return (
        spread(jnp.sum(token_pick, axis=1)).astype(jnp.bfloat16),
        spread(gate_terms).astype(jnp.float32),
        grad_in.astype(jnp.bfloat16)[None],
        grad_out.astype(jnp.bfloat16)[None],
    )


def per_device(tokens, out_grad, gates, expert_ids, w_in, w_out):
    plan = Plan(lax.axis_size("expert"), lax.axis_size("fsdp"), *tokens.shape)
    form = moved_rows if plan.fits() else all_rows
    return form(plan, tokens, out_grad, gates, expert_ids, w_in, w_out)


def solution(mesh):
    rows, both = P(("expert", "fsdp"), None), P("expert", None)
    weights = P("expert", None, "fsdp")
    return jax.shard_map(
        per_device,
        mesh=mesh,
        in_specs=(rows, rows, both, both, weights, weights),
        out_specs=(rows, rows, weights, weights),
        check_vma=False,
    )
```

```python
import functools

import jax
import jax.numpy as jnp
from jax import lax
from jax.experimental import pallas as pl
from jax.experimental.pallas import tpu as pltpu
from jax.sharding import PartitionSpec as P

COEF = 0.7978845608
CUBIC = 0.044715
ROW_DIMS = (((0,), (0,)), ((), ()))
LAST_DIMS = (((1,), (1,)), ((), ()))
LANES = 128
TILE = 8
PACK = 16
MIB = 1 << 20


def gelu_parts(pre_act):
    square = pre_act * pre_act
    half = 0.5 + 0.5 * jnp.tanh(pre_act * (COEF + (COEF * CUBIC) * square))
    values = pre_act * half
    slopes = half + values * ((1.0 - half) * (2.0 * COEF + (6.0 * COEF * CUBIC) * square))
    return values, slopes


def iota(shape, dim):
    return lax.broadcasted_iota(jnp.int32, shape, dim)


def one_hot(mask):
    return jnp.where(mask, 1.0, 0.0).astype(jnp.bfloat16)


class Plan:
    def __init__(self, experts, groups, tok_dev, width):
        self.experts, self.groups, self.tok_dev, self.width = experts, groups, tok_dev, width
        self.cap = 5 * tok_dev // (2 * experts)
        self.main = self.cap // PACK * PACK
        self.tail = self.cap - self.main
        self.send = 2 * self.cap
        self.back = self.main + TILE
        self.slots = experts * self.cap
        self.heads = experts * self.main

    def fits(self):
        return (
            self.groups == 2
            and self.main > 0
            and 2 * self.tail == TILE
            and self.cap <= LANES
            and self.tok_dev % LANES == 0
            and self.width % LANES == 0
        )


def dispatch_kernel(plan, ids_ref, gates_ref, x_ref, dy_ref, send_ref, route_ref):
    tokens = plan.tok_dev
    mine = pl.ds(pl.multiple_of(lax.axis_index("fsdp") * tokens, LANES), tokens)
    ids = ids_ref[:, mine]
    gates = gates_ref[:, mine].astype(jnp.float32)
    expert = iota((plan.experts, tokens), 0)
    named = [expert == ids[k : k + 1, :] for k in range(2)]
    earlier = one_hot(iota((tokens, tokens), 0) < iota((tokens, tokens), 1))
    counts = jnp.dot(one_hot(named[0] | named[1]), earlier, preferred_element_type=jnp.float32)
    row = iota((plan.experts * plan.send, tokens), 0)
    x_pick, dy_pick = False, 0.0
    for k in range(2):
        rank = jnp.sum(jnp.where(named[k], counts, 0.0), axis=0, keepdims=True).astype(jnp.int32)
        first = ids[k : k + 1, :] * plan.send + rank
        head = rank < plan.main
        x_pick = x_pick | (row == first + jnp.where(head, 0, plan.main))
        dy_pick = dy_pick + jnp.where(
            row == first + jnp.where(head, plan.main, plan.cap), gates[k : k + 1, :], 0.0
        )
        route_ref[k : k + 1, :] = ids[k : k + 1, :]
        route_ref[2 + k : 3 + k, :] = rank
        route_ref[4 + k : 5 + k, :] = jnp.zeros_like(rank)
        route_ref[6 + k : 7 + k, :] = jnp.zeros_like(rank)
    send = jnp.dot(one_hot(x_pick), x_ref[...], preferred_element_type=jnp.float32)
    send = send + jnp.dot(
        dy_pick.astype(jnp.bfloat16), dy_ref[...], preferred_element_type=jnp.float32
    )
    send_ref[...] = send.astype(jnp.bfloat16)


def unpack(plan, recv_ref, x_all, dy_all, at):
    main, tail, width = plan.main, plan.tail, plan.width
    tails = plan.experts * tail
    heads = pl.ds(at, plan.heads)
    x_all[heads, :] = recv_ref[:, :main, :].reshape(plan.heads, width)
    dy_all[heads, :] = recv_ref[:, main : 2 * main, :].reshape(plan.heads, width)
    mixed = recv_ref[:, 2 * main :, :].reshape(plan.experts * TILE, width)
    place, source = iota((2 * tails, plan.experts * TILE), 0), iota(
        (2 * tails, plan.experts * TILE), 1
    )
    second = jnp.where(place >= tails, 1, 0)
    slot = place - second * tails
    pick = one_hot(source == slot // tail * TILE + slot % tail + second * tail)
    split = jnp.dot(pick, mixed, preferred_element_type=jnp.float32).astype(jnp.bfloat16)
    x_all[pl.ds(at + plan.heads, tails), :] = split[:tails]
    dy_all[pl.ds(at + plan.heads, tails), :] = split[tails:]


def column_copies(sources, buffers, sems):
    block = buffers[0].shape[2]
    copies = []
    for pair in sources:
        for at in range(0, pair[0].shape[1], block):
            n = len(copies)
            copies.append(
                [
                    pltpu.make_async_copy(
                        ref.at[:, at : at + block], buffers[m].at[n], sems.at[m, n]
                    )
                    for m, ref in enumerate(pair)
                ]
            )
    return copies


def staged(count, ahead, finish):
    held = ahead(0)
    for n in range(count):
        later = ahead(n + 1) if n + 1 < count else None
        finish(n, *held)
        held = later


def first_acts(x_all, dy_all, buffers, copies, part):
    block = buffers[0].shape[2]

    def ahead(n):
        chunk, at = divmod(n * part, block)
        if at == 0:
            for copy in copies[chunk]:
                copy.wait()
        return tuple(
            jnp.dot(
                rows[...], mat[chunk, :, at : at + part], preferred_element_type=jnp.float32
            )
            for rows, mat in zip((x_all, dy_all), buffers)
        )

    return ahead


def token_kernel(
    plan, part, recv_ref, in_a, out_a, in_b, out_b, back_ref, x_all, dy_all, total, in_buf, out_buf, sems
):
    buffers = (in_buf, out_buf)
    copies = column_copies(((in_a, out_a), (in_b, out_b)), buffers, sems)
    for pair in copies:
        for copy in pair:
            copy.start()
    unpack(plan, recv_ref, x_all, dy_all, 0)
    block = in_buf.shape[2]
    gate_lanes = []

    def finish(n, pre_act, grad_act):
        chunk, at = divmod(n * part, block)
        values, slopes = gelu_parts(pre_act)
        grad_pre = (grad_act * slopes).astype(jnp.bfloat16)
        back = lax.dot_general(
            grad_pre,
            in_buf[chunk, :, at : at + part],
            LAST_DIMS,
            preferred_element_type=jnp.float32,
        )
        total[...] = back if n == 0 else total[...] + back
        product = grad_act * values
        for lane in range(0, part, LANES):
            piece = product[:, lane : lane + LANES]
            gate_lanes[:] = [gate_lanes[0] + piece] if gate_lanes else [piece]

    staged(len(copies) * block // part, first_acts(x_all, dy_all, buffers, copies, part), finish)

    main, tail, width = plan.main, plan.tail, plan.width
    tails = plan.experts * tail
    rows = total[...].astype(jnp.bfloat16)
    back_ref[:, :main, :] = rows[: plan.heads].reshape(plan.experts, main, width)
    gate = jnp.sum(gate_lanes[0], axis=1, keepdims=True)
    slot = iota((plan.slots, LANES), 0)
    over = slot - plan.heads
    rank = jnp.where(over >= 0, main + over % tail, slot % main)
    gate_rows = jnp.where(iota((plan.slots, LANES), 1) == rank, gate, 0.0).astype(jnp.bfloat16)
    place, slot = iota((plan.experts * TILE, plan.slots), 0), iota(
        (plan.experts * TILE, plan.slots), 1
    )
    over = slot - plan.heads
    source = jnp.where(over >= 0, over // tail, slot // main)
    gates = jnp.dot(
        one_hot(place == source * TILE + tail), gate_rows, preferred_element_type=jnp.float32
    )
    place, slot = iota((plan.experts * TILE, tails), 0), iota((plan.experts * TILE, tails), 1)
    rest = jnp.dot(
        one_hot(place == slot // tail * TILE + slot % tail),
        rows[plan.heads :],
        preferred_element_type=jnp.float32,
    )
    rest = jnp.concatenate([rest[:, :LANES] + gates, rest[:, LANES:]], axis=1)
    back_ref[:, main:, :] = rest.astype(jnp.bfloat16).reshape(plan.experts, TILE, width)


def weight_kernel(
    plan,
    part,
    own_ref,
    other_ref,
    in_ref,
    out_ref,
    grad_in_ref,
    grad_out_ref,
    x_all,
    dy_all,
    x_turned,
    dy_turned,
    in_buf,
    out_buf,
    in_grads,
    out_grads,
    sems,
    done,
):
    buffers = (in_buf, out_buf)
    copies = column_copies(((in_ref, out_ref),), buffers, sems)
    for pair in copies:
        for copy in pair:
            copy.start()
    unpack(plan, own_ref, x_all, dy_all, 0)
    unpack(plan, other_ref, x_all, dy_all, plan.slots)
    x_turned[...] = x_all[...].T
    dy_turned[...] = dy_all[...].T
    block = in_buf.shape[2]
    stores = []

    def finish(n, pre_act, grad_act):
        chunk, at = divmod(n * part, block)
        values, slopes = gelu_parts(pre_act)
        grad_pre = (grad_act * slopes).astype(jnp.bfloat16)
        for rows, acts, held in (
            (x_turned, grad_pre, in_grads),
            (dy_turned, values.astype(jnp.bfloat16), out_grads),
        ):
            held[chunk, :, at : at + part] = jnp.dot(
                rows[...], acts, preferred_element_type=jnp.float32
            ).astype(jnp.bfloat16)
        if at + part == block:
            columns = slice(chunk * block, (chunk + 1) * block)
            for m, (held, ref) in enumerate(((in_grads, grad_in_ref), (out_grads, grad_out_ref))):
                stores.append(
                    pltpu.make_async_copy(held.at[chunk], ref.at[:, columns], done.at[m, chunk])
                )
                stores[-1].start()

    staged(len(copies) * block // part, first_acts(x_all, dy_all, buffers, copies, part), finish)
    for store in stores:
        store.wait()


def combine_kernel(plan, route_ref, gates_ref, back_ref, token_ref, gate_ref):
    tokens, rows = plan.tok_dev, plan.experts * plan.back
    mine = pl.ds(pl.multiple_of(lax.axis_index("fsdp") * tokens, LANES), tokens)
    gates = gates_ref[:, mine].astype(jnp.float32)
    back = back_ref[...]
    row = iota((rows, tokens), 0)
    pick = False
    for k in range(2):
        pick = pick | (row == route_ref[k : k + 1, :] * plan.back + route_ref[2 + k : 3 + k, :])
    token_ref[...] = lax.dot_general(
        one_hot(pick), back, ROW_DIMS, preferred_element_type=jnp.float32
    ).astype(jnp.bfloat16)
    gate_row = iota((plan.experts, rows), 0) * plan.back + plan.cap
    gate_rows = jnp.dot(
        one_hot(iota((plan.experts, rows), 1) == gate_row),
        back[:, :LANES],
        preferred_element_type=jnp.float32,
    ).astype(jnp.bfloat16)
    for k in range(2):
        named = one_hot(iota((plan.experts, tokens), 0) == route_ref[k : k + 1, :])
        slots = lax.dot_general(gate_rows, named, ROW_DIMS, preferred_element_type=jnp.float32)
        here = iota((LANES, tokens), 0) == route_ref[2 + k : 3 + k, :]
        total = jnp.sum(jnp.where(here, slots, 0.0), axis=0, keepdims=True)
        gate_ref[k : k + 1, :] = total / gates[k : k + 1, :]


def params(mib):
    return pltpu.CompilerParams(vmem_limit_bytes=mib * MIB)


def moved_rows(plan, tokens, out_grad, gates, expert_ids, w_in, w_out):
    experts, width, slots = plan.experts, plan.width, plan.slots
    in_own, out_own = w_in[0], w_out[0]
    hidden = in_own.shape[1]
    swap = [(0, 1), (1, 0)]
    in_other = lax.ppermute(in_own, "fsdp", swap)
    out_other = lax.ppermute(out_own, "fsdp", swap)
    ids, gate_rows = expert_ids.T, gates.T
    bf16, f32 = jnp.bfloat16, jnp.float32

    send, route = pl.pallas_call(
        functools.partial(dispatch_kernel, plan),
        out_shape=(
            jax.ShapeDtypeStruct((experts * plan.send, width), bf16),
            jax.ShapeDtypeStruct((TILE, plan.tok_dev), jnp.int32),
        ),
        name="dispatch",
    )(ids, gate_rows, tokens, out_grad)
    recv = lax.all_to_all(
        send.reshape(experts, plan.send, width), "expert", split_axis=0, concat_axis=0, tiled=True
    )
    recv_other = lax.ppermute(recv, "fsdp", swap)

    block, part = min(512, hidden), min(256, hidden)
    blocks = hidden // block
    anywhere, held = pl.BlockSpec(memory_space=pl.ANY), pl.BlockSpec(memory_space=pltpu.VMEM)
    dma = pltpu.SemaphoreType.DMA

    def matrix(*shape):
        return pltpu.VMEM(shape, bf16)

    back = pl.pallas_call(
        functools.partial(token_kernel, plan, part),
        in_specs=[held] + [anywhere] * 4,
        out_specs=held,
        out_shape=jax.ShapeDtypeStruct((experts, plan.back, width), bf16),
        scratch_shapes=[
            matrix(slots, width),
            matrix(slots, width),
            pltpu.VMEM((slots, width), f32),
            matrix(2 * blocks, width, block),
            matrix(2 * blocks, width, block),
            dma((2, 2 * blocks)),
        ],
        cost_estimate=pl.CostEstimate(
            flops=12 * slots * width * hidden,
            transcendentals=2 * slots * hidden,
            bytes_accessed=8 * width * hidden,
        ),
        compiler_params=params(52),
        name="token_grad",
    )(recv, in_own, out_own, in_other, out_other)
    returned = lax.all_to_all(back, "expert", split_axis=0, concat_axis=0, tiled=True)

    grad_in, grad_out = pl.pallas_call(
        functools.partial(weight_kernel, plan, part),
        in_specs=[held, held, anywhere, anywhere],
        out_specs=(anywhere, anywhere),
        out_shape=(jax.ShapeDtypeStruct((width, hidden), bf16),) * 2,
        scratch_shapes=[
            matrix(2 * slots, width),
            matrix(2 * slots, width),
            matrix(width, 2 * slots),
            matrix(width, 2 * slots),
            matrix(blocks, width, block),
            matrix(blocks, width, block),
            matrix(blocks, width, block),
            matrix(blocks, width, block),
            dma((2, blocks)),
            dma((2, blocks)),
        ],
        cost_estimate=pl.CostEstimate(
            flops=16 * slots * width * hidden,
            transcendentals=2 * slots * hidden,
            bytes_accessed=8 * width * hidden,
        ),
        compiler_params=params(52),
        name="weight_grad",
    )(recv, recv_other, in_own, out_own)

    d_tokens, d_gates = pl.pallas_call(
        functools.partial(combine_kernel, plan),
        out_shape=(
            jax.ShapeDtypeStruct((plan.tok_dev, width), bf16),
            jax.ShapeDtypeStruct((2, plan.tok_dev), f32),
        ),
        compiler_params=params(16),
        name="combine",
    )(route, gate_rows, returned.reshape(experts * plan.back, width))
    return d_tokens, d_gates.T, grad_in[None], grad_out[None]


def slot_ranks(route_ids):
    count = route_ids.shape[1]
    same = route_ids[:, :, None] == route_ids[:, None, :]
    earlier = jnp.arange(count)[None, :] < jnp.arange(count)[:, None]
    return jnp.sum(jnp.logical_and(same, earlier[None]), axis=2)


def fill_slots(owner, rows_x, rows_dy, gate_flat):
    valid = owner >= 0
    safe = jnp.where(valid, owner, 0)
    token_row = safe // 2
    x_buf = jnp.where(valid[:, None], rows_x[token_row], jnp.zeros((), rows_x.dtype))
    dy_buf = jnp.where(valid[:, None], rows_dy[token_row], jnp.zeros((), rows_dy.dtype))
    gate_buf = jnp.where(valid, gate_flat[safe], jnp.zeros((), gate_flat.dtype))
    return (x_buf, dy_buf, gate_buf)


def expert_work(x_rows, dy_rows, gate_rows, in_shard, out_shard):
    pre_act = jnp.dot(x_rows, in_shard, preferred_element_type=jnp.float32)
    grad_act = jnp.dot(dy_rows, out_shard, preferred_element_type=jnp.float32)
    values, slopes = gelu_parts(pre_act)
    scale = gate_rows.astype(jnp.float32)[:, None]
    act_scaled = (scale * values).astype(jnp.bfloat16)
    grad_pre = (scale * grad_act * slopes).astype(jnp.bfloat16)
    grad_out = lax.dot_general(dy_rows, act_scaled, ROW_DIMS, preferred_element_type=jnp.float32)
    grad_in = lax.dot_general(x_rows, grad_pre, ROW_DIMS, preferred_element_type=jnp.float32)
    token_part = lax.dot_general(
        grad_pre, in_shard, LAST_DIMS, preferred_element_type=jnp.float32
    ).astype(jnp.bfloat16)
    gate_part = jnp.sum(grad_act * values, axis=1).astype(jnp.bfloat16)
    return (grad_in, grad_out, token_part, gate_part)


def all_rows(plan, tokens, out_grad, gates, expert_ids, w_in, w_out):
    tok_dev, width, groups = plan.tok_dev, plan.width, plan.groups
    experts, capacity = plan.experts, plan.cap
    group_ids = expert_ids.reshape(groups, 2 * tok_dev)
    group_gates = gates.reshape(groups, 2 * tok_dev)
    group_ranks = slot_ranks(group_ids)
    all_x = lax.all_gather(tokens, "fsdp", axis=0, tiled=True)
    all_dy = lax.all_gather(out_grad, "fsdp", axis=0, tiled=True)
    member = jnp.arange(groups, dtype=jnp.int32)[:, None]
    target = ((group_ids * groups + member) * capacity + group_ranks).reshape(-1)
    owner = (
        jnp.full((experts * groups * capacity,), -1, jnp.int32)
        .at[target]
        .set(jnp.arange(2 * tok_dev * groups, dtype=jnp.int32))
    )
    span = groups * capacity
    total_rows = experts * span

    def exchange(rows):
        rows = rows.reshape((experts, span) + rows.shape[1:])
        rows = lax.all_to_all(rows, "expert", split_axis=0, concat_axis=0, tiled=True)
        return rows.reshape((total_rows,) + rows.shape[2:])

    buffers = fill_slots(owner, all_x, all_dy, group_gates.reshape(-1))
    grad_in, grad_out, token_part, gate_part = expert_work(
        *(exchange(b) for b in buffers), w_in[0], w_out[0]
    )
    token_back, gate_back = exchange(token_part), exchange(gate_part)
    token_pick = token_back[target].astype(jnp.float32).reshape(groups * tok_dev, 2, width)
    gate_terms = gate_back[target].astype(jnp.float32).reshape(groups * tok_dev, 2)

    def spread(terms):
        return lax.psum_scatter(
            terms.astype(jnp.bfloat16), "fsdp", scatter_dimension=0, tiled=True
        )

    return (
        spread(jnp.sum(token_pick, axis=1)).astype(jnp.bfloat16),
        spread(gate_terms).astype(jnp.float32),
        grad_in.astype(jnp.bfloat16)[None],
        grad_out.astype(jnp.bfloat16)[None],
    )


def per_device(tokens, out_grad, gates, expert_ids, w_in, w_out):
    plan = Plan(lax.axis_size("expert"), lax.axis_size("fsdp"), *tokens.shape)
    form = moved_rows if plan.fits() else all_rows
    return form(plan, tokens, out_grad, gates, expert_ids, w_in, w_out)


def solution(mesh):
    rows, both = P(("expert", "fsdp"), None), P("expert", None)
    weights = P("expert", None, "fsdp")
    return jax.shard_map(
        per_device,
        mesh=mesh,
        in_specs=(rows, rows, both, both, weights, weights),
        out_specs=(rows, rows, weights, weights),
        check_vma=False,
    )
```

```python
import functools

import jax
import jax.numpy as jnp
from jax import lax
from jax.experimental import pallas as pl
from jax.experimental.pallas import tpu as pltpu
from jax.sharding import PartitionSpec as P


COEF = 0.7978845608
CUBIC = 0.044715
ROW_DIMS = (((0,), (0,)), ((), ()))
LAST_DIMS = (((1,), (1,)), ((), ()))
LANES = 128
TILE = 8
PACK = 16
MIB = 1 << 20


def gelu_parts(pre_act):
    square = pre_act * pre_act
    half = 0.5 + 0.5 * jnp.tanh(pre_act * (COEF + (COEF * CUBIC) * square))
    values = pre_act * half
    slopes = half + values * ((1.0 - half) * (2.0 * COEF + (6.0 * COEF * CUBIC) * square))
    return values, slopes


def iota(shape, dim):
    return lax.broadcasted_iota(jnp.int32, shape, dim)


def one_hot(mask):
    return jnp.where(mask, 1.0, 0.0).astype(jnp.bfloat16)


class Plan:
    def __init__(self, experts, groups, tok_dev, width):
        self.experts, self.groups, self.tok_dev, self.width = experts, groups, tok_dev, width
        self.cap = 5 * tok_dev // (2 * experts)
        self.main = self.cap // PACK * PACK
        self.tail = self.cap - self.main
        self.send = 2 * self.cap
        self.back = self.main + TILE
        self.slots = experts * self.cap
        self.heads = experts * self.main

    def fits(self):
        return (
            self.groups == 2
            and self.main > 0
            and 2 * self.tail == TILE
            and self.cap <= LANES
            and self.tok_dev % LANES == 0
            and self.width % LANES == 0
        )


def dispatch_kernel(plan, ids_ref, gates_ref, x_ref, dy_ref, send_ref, route_ref):
    tokens = plan.tok_dev
    mine = pl.ds(pl.multiple_of(lax.axis_index("fsdp") * tokens, LANES), tokens)
    ids = ids_ref[:, mine]
    gates = gates_ref[:, mine].astype(jnp.float32)
    expert = iota((plan.experts, tokens), 0)
    named = [expert == ids[k : k + 1, :] for k in range(2)]
    earlier = one_hot(iota((tokens, tokens), 0) < iota((tokens, tokens), 1))
    counts = jnp.dot(one_hot(named[0] | named[1]), earlier, preferred_element_type=jnp.float32)
    row = iota((plan.experts * plan.send, tokens), 0)
    x_pick, dy_pick = False, 0.0
    for k in range(2):
        rank = jnp.sum(jnp.where(named[k], counts, 0.0), axis=0, keepdims=True).astype(jnp.int32)
        first = ids[k : k + 1, :] * plan.send + rank
        head = rank < plan.main
        x_pick = x_pick | (row == first + jnp.where(head, 0, plan.main))
        dy_pick = dy_pick + jnp.where(
            row == first + jnp.where(head, plan.main, plan.cap), gates[k : k + 1, :], 0.0
        )
        route_ref[k : k + 1, :] = ids[k : k + 1, :]
        route_ref[2 + k : 3 + k, :] = rank
        route_ref[4 + k : 5 + k, :] = jnp.zeros_like(rank)
        route_ref[6 + k : 7 + k, :] = jnp.zeros_like(rank)
    send = jnp.dot(one_hot(x_pick), x_ref[...], preferred_element_type=jnp.float32)
    send = send + jnp.dot(
        dy_pick.astype(jnp.bfloat16), dy_ref[...], preferred_element_type=jnp.float32
    )
    send_ref[...] = send.astype(jnp.bfloat16)


def unpack(plan, recv_ref, x_all, dy_all, at):
    main, tail, width = plan.main, plan.tail, plan.width
    tails = plan.experts * tail
    heads = pl.ds(at, plan.heads)
    x_all[heads, :] = recv_ref[:, :main, :].reshape(plan.heads, width)
    dy_all[heads, :] = recv_ref[:, main : 2 * main, :].reshape(plan.heads, width)
    mixed = recv_ref[:, 2 * main :, :].reshape(plan.experts * TILE, width)
    place, source = iota((2 * tails, plan.experts * TILE), 0), iota(
        (2 * tails, plan.experts * TILE), 1
    )
    second = jnp.where(place >= tails, 1, 0)
    slot = place - second * tails
    pick = one_hot(source == slot // tail * TILE + slot % tail + second * tail)
    split = jnp.dot(pick, mixed, preferred_element_type=jnp.float32).astype(jnp.bfloat16)
    x_all[pl.ds(at + plan.heads, tails), :] = split[:tails]
    dy_all[pl.ds(at + plan.heads, tails), :] = split[tails:]


def column_copies(sources, buffers, sems):
    block = buffers[0].shape[2]
    copies = []
    for pair in sources:
        for at in range(0, pair[0].shape[1], block):
            n = len(copies)
            copies.append(
                [
                    pltpu.make_async_copy(
                        ref.at[:, at : at + block], buffers[m].at[n], sems.at[m, n]
                    )
                    for m, ref in enumerate(pair)
                ]
            )
    return copies


def staged(count, ahead, finish):
    held = ahead(0)
    for n in range(count):
        later = ahead(n + 1) if n + 1 < count else None
        finish(n, *held)
        held = later


def first_acts(x_all, dy_all, buffers, copies, part):
    block = buffers[0].shape[2]

    def ahead(n):
        chunk, at = divmod(n * part, block)
        if at == 0:
            for copy in copies[chunk]:
                copy.wait()
        return tuple(
            jnp.dot(
                rows[...], mat[chunk, :, at : at + part], preferred_element_type=jnp.float32
            )
            for rows, mat in zip((x_all, dy_all), buffers)
        )

    return ahead


def token_kernel(
    plan, part, recv_ref, in_a, out_a, in_b, out_b, back_ref, x_all, dy_all, total, in_buf, out_buf, sems
):
    buffers = (in_buf, out_buf)
    copies = column_copies(((in_a, out_a), (in_b, out_b)), buffers, sems)
    for pair in copies:
        for copy in pair:
            copy.start()
    unpack(plan, recv_ref, x_all, dy_all, 0)
    block = in_buf.shape[2]
    gate_lanes = []

    def finish(n, pre_act, grad_act):
        chunk, at = divmod(n * part, block)
        values, slopes = gelu_parts(pre_act)
        grad_pre = (grad_act * slopes).astype(jnp.bfloat16)
        back = lax.dot_general(
            grad_pre,
            in_buf[chunk, :, at : at + part],
            LAST_DIMS,
            preferred_element_type=jnp.float32,
        )
        total[...] = back if n == 0 else total[...] + back
        product = grad_act * values
        for lane in range(0, part, LANES):
            piece = product[:, lane : lane + LANES]
            gate_lanes[:] = [gate_lanes[0] + piece] if gate_lanes else [piece]

    staged(len(copies) * block // part, first_acts(x_all, dy_all, buffers, copies, part), finish)

    main, tail, width = plan.main, plan.tail, plan.width
    tails = plan.experts * tail
    rows = total[...].astype(jnp.bfloat16)
    back_ref[:, :main, :] = rows[: plan.heads].reshape(plan.experts, main, width)
    gate = jnp.sum(gate_lanes[0], axis=1, keepdims=True)
    slot = iota((plan.slots, LANES), 0)
    over = slot - plan.heads
    rank = jnp.where(over >= 0, main + over % tail, slot % main)
    gate_rows = jnp.where(iota((plan.slots, LANES), 1) == rank, gate, 0.0).astype(jnp.bfloat16)
    place, slot = iota((plan.experts * TILE, plan.slots), 0), iota(
        (plan.experts * TILE, plan.slots), 1
    )
    over = slot - plan.heads
    source = jnp.where(over >= 0, over // tail, slot // main)
    gates = jnp.dot(
        one_hot(place == source * TILE + tail), gate_rows, preferred_element_type=jnp.float32
    )
    place, slot = iota((plan.experts * TILE, tails), 0), iota((plan.experts * TILE, tails), 1)
    rest = jnp.dot(
        one_hot(place == slot // tail * TILE + slot % tail),
        rows[plan.heads :],
        preferred_element_type=jnp.float32,
    )
    rest = jnp.concatenate([rest[:, :LANES] + gates, rest[:, LANES:]], axis=1)
    back_ref[:, main:, :] = rest.astype(jnp.bfloat16).reshape(plan.experts, TILE, width)


def weight_kernel(
    plan,
    part,
    own_ref,
    other_ref,
    in_ref,
    out_ref,
    grad_in_ref,
    grad_out_ref,
    x_all,
    dy_all,
    x_turned,
    dy_turned,
    in_buf,
    out_buf,
    in_grads,
    out_grads,
    sems,
    done,
):
    buffers = (in_buf, out_buf)
    copies = column_copies(((in_ref, out_ref),), buffers, sems)
    for pair in copies:
        for copy in pair:
            copy.start()
    unpack(plan, own_ref, x_all, dy_all, 0)
    unpack(plan, other_ref, x_all, dy_all, plan.slots)
    x_turned[...] = x_all[...].T
    dy_turned[...] = dy_all[...].T
    block = in_buf.shape[2]
    stores = []

    def finish(n, pre_act, grad_act):
        chunk, at = divmod(n * part, block)
        values, slopes = gelu_parts(pre_act)
        grad_pre = (grad_act * slopes).astype(jnp.bfloat16)
        for rows, acts, held in (
            (x_turned, grad_pre, in_grads),
            (dy_turned, values.astype(jnp.bfloat16), out_grads),
        ):
            held[chunk, :, at : at + part] = jnp.dot(
                rows[...], acts, preferred_element_type=jnp.float32
            ).astype(jnp.bfloat16)
        if at + part == block:
            columns = slice(chunk * block, (chunk + 1) * block)
            for m, (held, ref) in enumerate(((in_grads, grad_in_ref), (out_grads, grad_out_ref))):
                stores.append(
                    pltpu.make_async_copy(held.at[chunk], ref.at[:, columns], done.at[m, chunk])
                )
                stores[-1].start()

    staged(len(copies) * block // part, first_acts(x_all, dy_all, buffers, copies, part), finish)
    for store in stores:
        store.wait()


def place_kernel(plan, route_ref, pick_ref):
    row = iota((plan.experts * plan.back, plan.tok_dev), 0)
    pick = False
    for k in range(2):
        pick = pick | (row == route_ref[k : k + 1, :] * plan.back + route_ref[2 + k : 3 + k, :])
    pick_ref[...] = jnp.where(pick, 1.0, 0.0).T.astype(jnp.bfloat16)


def combine_kernel(plan, route_ref, pick_ref, gates_ref, back_ref, token_ref, gate_ref):
    tokens, rows = plan.tok_dev, plan.experts * plan.back
    mine = pl.ds(pl.multiple_of(lax.axis_index("fsdp") * tokens, LANES), tokens)
    gates = gates_ref[:, mine].astype(jnp.float32)
    back = back_ref[...]
    token_ref[...] = jnp.dot(
        pick_ref[...], back, preferred_element_type=jnp.float32
    ).astype(jnp.bfloat16)
    gate_row = iota((plan.experts, rows), 0) * plan.back + plan.cap
    gate_rows = jnp.dot(
        one_hot(iota((plan.experts, rows), 1) == gate_row),
        back[:, :LANES],
        preferred_element_type=jnp.float32,
    ).astype(jnp.bfloat16)
    for k in range(2):
        named = one_hot(iota((plan.experts, tokens), 0) == route_ref[k : k + 1, :])
        slots = lax.dot_general(gate_rows, named, ROW_DIMS, preferred_element_type=jnp.float32)
        here = iota((LANES, tokens), 0) == route_ref[2 + k : 3 + k, :]
        total = jnp.sum(jnp.where(here, slots, 0.0), axis=0, keepdims=True)
        gate_ref[k : k + 1, :] = total / gates[k : k + 1, :]


def params(mib):
    return pltpu.CompilerParams(vmem_limit_bytes=mib * MIB)


def moved_rows(plan, tokens, out_grad, gates, expert_ids, w_in, w_out):
    experts, width, slots = plan.experts, plan.width, plan.slots
    in_own, out_own = w_in[0], w_out[0]
    hidden = in_own.shape[1]
    swap = [(0, 1), (1, 0)]
    in_other = lax.ppermute(in_own, "fsdp", swap)
    out_other = lax.ppermute(out_own, "fsdp", swap)
    ids, gate_rows = expert_ids.T, gates.T
    bf16, f32 = jnp.bfloat16, jnp.float32

    send, route = pl.pallas_call(
        functools.partial(dispatch_kernel, plan),
        out_shape=(
            jax.ShapeDtypeStruct((experts * plan.send, width), bf16),
            jax.ShapeDtypeStruct((TILE, plan.tok_dev), jnp.int32),
        ),
        name="dispatch",
    )(ids, gate_rows, tokens, out_grad)
    recv = lax.all_to_all(
        send.reshape(experts, plan.send, width),
        "expert",
        split_axis=0,
        concat_axis=0,
        tiled=True,
    )
    recv_other = lax.ppermute(recv, "fsdp", swap)
    pick = pl.pallas_call(
        functools.partial(place_kernel, plan),
        out_shape=jax.ShapeDtypeStruct((plan.tok_dev, experts * plan.back), bf16),
        compiler_params=params(63),
        name="placing",
    )(route)

    block, part = min(256, hidden), min(256, hidden)
    blocks = hidden // block
    anywhere, held = pl.BlockSpec(memory_space=pl.ANY), pl.BlockSpec(memory_space=pltpu.VMEM)
    dma = pltpu.SemaphoreType.DMA

    def matrix(*shape):
        return pltpu.VMEM(shape, bf16)

    back = pl.pallas_call(
        functools.partial(token_kernel, plan, part),
        in_specs=[held] + [anywhere] * 4,
        out_specs=held,
        out_shape=jax.ShapeDtypeStruct((experts, plan.back, width), bf16),
        scratch_shapes=[
            matrix(slots, width),
            matrix(slots, width),
            pltpu.VMEM((slots, width), f32),
            matrix(2 * blocks, width, block),
            matrix(2 * blocks, width, block),
            dma((2, 2 * blocks)),
        ],
        cost_estimate=pl.CostEstimate(
            flops=12 * slots * width * hidden,
            transcendentals=2 * slots * hidden,
            bytes_accessed=8 * width * hidden,
        ),
        compiler_params=params(52),
        name="token_grad",
    )(recv, in_own, out_own, in_other, out_other)
    returned = lax.all_to_all(back, "expert", split_axis=0, concat_axis=0, tiled=True)

    grad_in, grad_out = pl.pallas_call(
        functools.partial(weight_kernel, plan, part),
        in_specs=[held, held, anywhere, anywhere],
        out_specs=(anywhere, anywhere),
        out_shape=(jax.ShapeDtypeStruct((width, hidden), bf16),) * 2,
        scratch_shapes=[
            matrix(2 * slots, width),
            matrix(2 * slots, width),
            matrix(width, 2 * slots),
            matrix(width, 2 * slots),
            matrix(blocks, width, block),
            matrix(blocks, width, block),
            matrix(blocks, width, block),
            matrix(blocks, width, block),
            dma((2, blocks)),
            dma((2, blocks)),
        ],
        cost_estimate=pl.CostEstimate(
            flops=16 * slots * width * hidden,
            transcendentals=2 * slots * hidden,
            bytes_accessed=8 * width * hidden,
        ),
        compiler_params=params(52),
        name="weight_grad",
    )(recv, recv_other, in_own, out_own)

    d_tokens, d_gates = pl.pallas_call(
        functools.partial(combine_kernel, plan),
        out_shape=(
            jax.ShapeDtypeStruct((plan.tok_dev, width), bf16),
            jax.ShapeDtypeStruct((2, plan.tok_dev), f32),
        ),
        compiler_params=params(16),
        name="combine",
    )(route, pick, gate_rows, returned.reshape(experts * plan.back, width))
    return d_tokens, d_gates.T, grad_in[None], grad_out[None]


def slot_ranks(route_ids):
    count = route_ids.shape[1]
    same = route_ids[:, :, None] == route_ids[:, None, :]
    earlier = jnp.arange(count)[None, :] < jnp.arange(count)[:, None]
    return jnp.sum(jnp.logical_and(same, earlier[None]), axis=2)


def fill_slots(owner, rows_x, rows_dy, gate_flat):
    valid = owner >= 0
    safe = jnp.where(valid, owner, 0)
    token_row = safe // 2
    x_buf = jnp.where(valid[:, None], rows_x[token_row], jnp.zeros((), rows_x.dtype))
    dy_buf = jnp.where(valid[:, None], rows_dy[token_row], jnp.zeros((), rows_dy.dtype))
    gate_buf = jnp.where(valid, gate_flat[safe], jnp.zeros((), gate_flat.dtype))
    return (x_buf, dy_buf, gate_buf)


def expert_work(x_rows, dy_rows, gate_rows, in_shard, out_shard):
    pre_act = jnp.dot(x_rows, in_shard, preferred_element_type=jnp.float32)
    grad_act = jnp.dot(dy_rows, out_shard, preferred_element_type=jnp.float32)
    values, slopes = gelu_parts(pre_act)
    scale = gate_rows.astype(jnp.float32)[:, None]
    act_scaled = (scale * values).astype(jnp.bfloat16)
    grad_pre = (scale * grad_act * slopes).astype(jnp.bfloat16)
    grad_out = lax.dot_general(dy_rows, act_scaled, ROW_DIMS, preferred_element_type=jnp.float32)
    grad_in = lax.dot_general(x_rows, grad_pre, ROW_DIMS, preferred_element_type=jnp.float32)
    token_part = lax.dot_general(
        grad_pre, in_shard, LAST_DIMS, preferred_element_type=jnp.float32
    ).astype(jnp.bfloat16)
    gate_part = jnp.sum(grad_act * values, axis=1).astype(jnp.bfloat16)
    return (grad_in, grad_out, token_part, gate_part)


def all_rows(plan, tokens, out_grad, gates, expert_ids, w_in, w_out):
    tok_dev, width, groups = plan.tok_dev, plan.width, plan.groups
    experts, capacity = plan.experts, plan.cap
    group_ids = expert_ids.reshape(groups, 2 * tok_dev)
    group_gates = gates.reshape(groups, 2 * tok_dev)
    group_ranks = slot_ranks(group_ids)
    all_x = lax.all_gather(tokens, "fsdp", axis=0, tiled=True)
    all_dy = lax.all_gather(out_grad, "fsdp", axis=0, tiled=True)
    member = jnp.arange(groups, dtype=jnp.int32)[:, None]
    target = ((group_ids * groups + member) * capacity + group_ranks).reshape(-1)
    owner = (
        jnp.full((experts * groups * capacity,), -1, jnp.int32)
        .at[target]
        .set(jnp.arange(2 * tok_dev * groups, dtype=jnp.int32))
    )
    span = groups * capacity
    total_rows = experts * span

    def exchange(rows):
        rows = rows.reshape((experts, span) + rows.shape[1:])
        rows = lax.all_to_all(rows, "expert", split_axis=0, concat_axis=0, tiled=True)
        return rows.reshape((total_rows,) + rows.shape[2:])

    buffers = fill_slots(owner, all_x, all_dy, group_gates.reshape(-1))
    grad_in, grad_out, token_part, gate_part = expert_work(
        *(exchange(b) for b in buffers), w_in[0], w_out[0]
    )
    token_back, gate_back = exchange(token_part), exchange(gate_part)
    token_pick = token_back[target].astype(jnp.float32).reshape(groups * tok_dev, 2, width)
    gate_terms = gate_back[target].astype(jnp.float32).reshape(groups * tok_dev, 2)

    def spread(terms):
        return lax.psum_scatter(
            terms.astype(jnp.bfloat16), "fsdp", scatter_dimension=0, tiled=True
        )

    return (
        spread(jnp.sum(token_pick, axis=1)).astype(jnp.bfloat16),
        spread(gate_terms).astype(jnp.float32),
        grad_in.astype(jnp.bfloat16)[None],
        grad_out.astype(jnp.bfloat16)[None],
    )


def per_device(tokens, out_grad, gates, expert_ids, w_in, w_out):
    plan = Plan(lax.axis_size("expert"), lax.axis_size("fsdp"), *tokens.shape)
    form = moved_rows if plan.fits() else all_rows
    return form(plan, tokens, out_grad, gates, expert_ids, w_in, w_out)


def solution(mesh):
    rows, both = P(("expert", "fsdp"), None), P("expert", None)
    weights = P("expert", None, "fsdp")
    return jax.shard_map(
        per_device,
        mesh=mesh,
        in_specs=(rows, rows, both, both, weights, weights),
        out_specs=(rows, rows, weights, weights),
        check_vma=False,
    )
```

```python
import functools

import jax
import jax.numpy as jnp
from jax import lax
from jax.experimental import pallas as pl
from jax.experimental.pallas import tpu as pltpu
from jax.sharding import PartitionSpec as P


COEF = 0.7978845608
CUBIC = 0.044715
ROW_DIMS = (((0,), (0,)), ((), ()))
LAST_DIMS = (((1,), (1,)), ((), ()))
LANES = 128
TILE = 8
PACK = 16
MIB = 1 << 20


def gelu_parts(pre_act):
    square = pre_act * pre_act
    half = 0.5 + 0.5 * jnp.tanh(pre_act * (COEF + (COEF * CUBIC) * square))
    values = pre_act * half
    slopes = half + values * ((1.0 - half) * (2.0 * COEF + (6.0 * COEF * CUBIC) * square))
    return values, slopes


def iota(shape, dim):
    return lax.broadcasted_iota(jnp.int32, shape, dim)


def one_hot(mask):
    return jnp.where(mask, 1.0, 0.0).astype(jnp.bfloat16)


class Plan:
    def __init__(self, experts, groups, tok_dev, width):
        self.experts, self.groups, self.tok_dev, self.width = experts, groups, tok_dev, width
        self.cap = 5 * tok_dev // (2 * experts)
        self.main = self.cap // PACK * PACK
        self.tail = self.cap - self.main
        self.send = 2 * self.cap
        self.back = self.main + TILE
        self.slots = experts * self.cap
        self.heads = experts * self.main

    def fits(self):
        return (
            self.groups == 2
            and self.main == PACK
            and 2 * self.tail == TILE
            and self.cap <= LANES
            and self.tok_dev % LANES == 0
            and self.width % LANES == 0
        )


def dispatch_kernel(plan, ids_ref, gates_ref, x_ref, dy_ref, send_ref, route_ref):
    tokens = plan.tok_dev
    mine = pl.ds(pl.multiple_of(lax.axis_index("fsdp") * tokens, LANES), tokens)
    ids = ids_ref[:, mine]
    gates = gates_ref[:, mine].astype(jnp.float32)
    expert = iota((plan.experts, tokens), 0)
    named = [expert == ids[k : k + 1, :] for k in range(2)]
    earlier = one_hot(iota((tokens, tokens), 0) < iota((tokens, tokens), 1))
    counts = jnp.dot(one_hot(named[0] | named[1]), earlier, preferred_element_type=jnp.float32)
    row = iota((plan.experts * plan.send, tokens), 0)
    x_pick, dy_pick = False, 0.0
    for k in range(2):
        rank = jnp.sum(jnp.where(named[k], counts, 0.0), axis=0, keepdims=True).astype(jnp.int32)
        first = ids[k : k + 1, :] * plan.send + rank
        head = rank < plan.main
        x_pick = x_pick | (row == first + jnp.where(head, 0, plan.main))
        dy_pick = dy_pick + jnp.where(
            row == first + jnp.where(head, plan.main, plan.cap), gates[k : k + 1, :], 0.0
        )
        route_ref[k : k + 1, :] = ids[k : k + 1, :]
        route_ref[2 + k : 3 + k, :] = rank
        route_ref[4 + k : 5 + k, :] = jnp.zeros_like(rank)
        route_ref[6 + k : 7 + k, :] = jnp.zeros_like(rank)
    send = jnp.dot(one_hot(x_pick), x_ref[...], preferred_element_type=jnp.float32)
    send = send + jnp.dot(
        dy_pick.astype(jnp.bfloat16), dy_ref[...], preferred_element_type=jnp.float32
    )
    send_ref[...] = send.astype(jnp.bfloat16)


def unpack(plan, recv_ref, x_all, dy_all, at):
    main, tail, width = plan.main, plan.tail, plan.width
    tails = plan.experts * tail
    heads = pl.ds(at, plan.heads)
    x_all[heads, :] = recv_ref[:, :main, :].reshape(plan.heads, width)
    dy_all[heads, :] = recv_ref[:, main : 2 * main, :].reshape(plan.heads, width)
    mixed = recv_ref[:, 2 * main :, :].reshape(plan.experts * TILE, width)
    place, source = iota((2 * tails, plan.experts * TILE), 0), iota(
        (2 * tails, plan.experts * TILE), 1
    )
    second = jnp.where(place >= tails, 1, 0)
    slot = place - second * tails
    pick = one_hot(source == slot // tail * TILE + slot % tail + second * tail)
    split = jnp.dot(pick, mixed, preferred_element_type=jnp.float32).astype(jnp.bfloat16)
    x_all[pl.ds(at + plan.heads, tails), :] = split[:tails]
    dy_all[pl.ds(at + plan.heads, tails), :] = split[tails:]


def stage_kernel(_, in_hbm, out_hbm, in_first, out_first, sems):
    columns = slice(0, in_first.shape[1])
    copies = [
        pltpu.make_async_copy(ref.at[:, columns], first, sems.at[m])
        for m, (ref, first) in enumerate(((in_hbm, in_first), (out_hbm, out_first)))
    ]
    for copy in copies:
        copy.start()
    for copy in copies:
        copy.wait()


def column_copies(sources, buffers, sems):
    block = buffers[0].shape[2]
    copies = []
    for pair in sources:
        for at in range(0, pair[0].shape[1], block):
            n = len(copies)
            copies.append(
                [
                    pltpu.make_async_copy(
                        ref.at[:, at : at + block], buffers[m].at[n], sems.at[m, n]
                    )
                    for m, ref in enumerate(pair)
                ]
            )
    return copies


def staged(count, ahead, finish):
    held = ahead(0)
    for n in range(count):
        later = ahead(n + 1) if n + 1 < count else None
        finish(n, *held)
        held = later


def part_of(first, buffer, n, part):
    chunk, at = divmod(n * part, buffer.shape[2])
    return first[:, at : at + part] if chunk == 0 else buffer[chunk, :, at : at + part]


def first_acts(x_all, dy_all, firsts, buffers, copies, part):
    block = buffers[0].shape[2]

    def ahead(n):
        chunk, at = divmod(n * part, block)
        if at == 0 and chunk > 0:
            for copy in copies[chunk]:
                copy.wait()
        return tuple(
            jnp.dot(
                rows[...], part_of(first, mat, n, part), preferred_element_type=jnp.float32
            )
            for rows, first, mat in zip((x_all, dy_all), firsts, buffers)
        )

    return ahead


def token_kernel(
    plan, part, recv_ref, in_first, out_first, in_a, out_a, in_b, out_b, back_ref, x_all, dy_all, total, in_buf, out_buf, sems
):
    buffers, firsts = (in_buf, out_buf), (in_first, out_first)
    copies = column_copies(((in_a, out_a), (in_b, out_b)), buffers, sems)
    for pair in copies[1:]:
        for copy in pair:
            copy.start()
    unpack(plan, recv_ref, x_all, dy_all, 0)
    block = in_buf.shape[2]
    gate_lanes = []

    def finish(n, pre_act, grad_act):
        values, slopes = gelu_parts(pre_act)
        grad_pre = (grad_act * slopes).astype(jnp.bfloat16)
        back = lax.dot_general(
            grad_pre,
            part_of(in_first, in_buf, n, part),
            LAST_DIMS,
            preferred_element_type=jnp.float32,
        )
        total[...] = back if n == 0 else total[...] + back
        product = grad_act * values
        for lane in range(0, part, LANES):
            piece = product[:, lane : lane + LANES]
            gate_lanes[:] = [gate_lanes[0] + piece] if gate_lanes else [piece]

    staged(len(copies) * block // part, first_acts(x_all, dy_all, firsts, buffers, copies, part), finish)

    main, tail, width = plan.main, plan.tail, plan.width
    tails = plan.experts * tail
    rows = total[...].astype(jnp.bfloat16)
    back_ref[:, :main, :] = rows[: plan.heads].reshape(plan.experts, main, width)
    gate = jnp.sum(gate_lanes[0], axis=1, keepdims=True)
    slot = iota((plan.slots, LANES), 0)
    over = slot - plan.heads
    rank = jnp.where(over >= 0, main + over % tail, slot % main)
    gate_rows = jnp.where(iota((plan.slots, LANES), 1) == rank, gate, 0.0).astype(jnp.bfloat16)
    place, slot = iota((plan.experts * TILE, plan.slots), 0), iota(
        (plan.experts * TILE, plan.slots), 1
    )
    over = slot - plan.heads
    source = jnp.where(over >= 0, over // tail, slot // main)
    gates = jnp.dot(
        one_hot(place == source * TILE + tail), gate_rows, preferred_element_type=jnp.float32
    )
    place, slot = iota((plan.experts * TILE, tails), 0), iota((plan.experts * TILE, tails), 1)
    rest = jnp.dot(
        one_hot(place == slot // tail * TILE + slot % tail),
        rows[plan.heads :],
        preferred_element_type=jnp.float32,
    )
    rest = jnp.concatenate([rest[:, :LANES] + gates, rest[:, LANES:]], axis=1)
    back_ref[:, main:, :] = rest.astype(jnp.bfloat16).reshape(plan.experts, TILE, width)


def weight_kernel(
    plan,
    part,
    own_ref,
    other_ref,
    in_first,
    out_first,
    in_ref,
    out_ref,
    grad_in_ref,
    grad_out_ref,
    x_all,
    dy_all,
    x_turned,
    dy_turned,
    in_buf,
    out_buf,
    in_grads,
    out_grads,
    sems,
    done,
):
    buffers, firsts = (in_buf, out_buf), (in_first, out_first)
    copies = column_copies(((in_ref, out_ref),), buffers, sems)
    for pair in copies[1:]:
        for copy in pair:
            copy.start()
    unpack(plan, own_ref, x_all, dy_all, 0)
    unpack(plan, other_ref, x_all, dy_all, plan.slots)
    x_turned[...] = x_all[...].T
    dy_turned[...] = dy_all[...].T
    block = in_buf.shape[2]
    stores = []

    def finish(n, pre_act, grad_act):
        chunk, at = divmod(n * part, block)
        values, slopes = gelu_parts(pre_act)
        grad_pre = (grad_act * slopes).astype(jnp.bfloat16)
        for rows, acts, held in (
            (x_turned, grad_pre, in_grads),
            (dy_turned, values.astype(jnp.bfloat16), out_grads),
        ):
            held[chunk, :, at : at + part] = jnp.dot(
                rows[...], acts, preferred_element_type=jnp.float32
            ).astype(jnp.bfloat16)
        if at + part == block:
            columns = slice(chunk * block, (chunk + 1) * block)
            for m, (held, ref) in enumerate(((in_grads, grad_in_ref), (out_grads, grad_out_ref))):
                stores.append(
                    pltpu.make_async_copy(held.at[chunk], ref.at[:, columns], done.at[m, chunk])
                )
                stores[-1].start()

    staged(len(copies) * block // part, first_acts(x_all, dy_all, firsts, buffers, copies, part), finish)
    for store in stores:
        store.wait()


def place_kernel(plan, route_ref, pick_ref):
    row = iota((plan.experts * plan.back, plan.tok_dev), 0)
    pick = False
    for k in range(2):
        pick = pick | (row == route_ref[k : k + 1, :] * plan.back + route_ref[2 + k : 3 + k, :])
    pick_ref[...] = jnp.where(pick, 1.0, 0.0).T.astype(jnp.bfloat16)


def combine_kernel(plan, route_ref, pick_ref, gates_ref, back_ref, token_ref, gate_ref):
    tokens, rows = plan.tok_dev, plan.experts * plan.back
    mine = pl.ds(pl.multiple_of(lax.axis_index("fsdp") * tokens, LANES), tokens)
    gates = gates_ref[:, mine].astype(jnp.float32)
    back = back_ref[...]
    token_ref[...] = jnp.dot(
        pick_ref[...], back, preferred_element_type=jnp.float32
    ).astype(jnp.bfloat16)
    gate_row = iota((plan.experts, rows), 0) * plan.back + plan.cap
    gate_rows = jnp.dot(
        one_hot(iota((plan.experts, rows), 1) == gate_row),
        back[:, :LANES],
        preferred_element_type=jnp.float32,
    ).astype(jnp.bfloat16)
    for k in range(2):
        named = one_hot(iota((plan.experts, tokens), 0) == route_ref[k : k + 1, :])
        slots = lax.dot_general(gate_rows, named, ROW_DIMS, preferred_element_type=jnp.float32)
        here = iota((LANES, tokens), 0) == route_ref[2 + k : 3 + k, :]
        total = jnp.sum(jnp.where(here, slots, 0.0), axis=0, keepdims=True)
        gate_ref[k : k + 1, :] = total / gates[k : k + 1, :]


def params(mib):
    return pltpu.CompilerParams(vmem_limit_bytes=mib * MIB)


def moved_rows(plan, tokens, out_grad, gates, expert_ids, w_in, w_out):
    experts, width, slots = plan.experts, plan.width, plan.slots
    in_own, out_own = w_in[0], w_out[0]
    hidden = in_own.shape[1]
    swap = [(0, 1), (1, 0)]
    in_other = lax.ppermute(in_own, "fsdp", swap)
    out_other = lax.ppermute(out_own, "fsdp", swap)
    ids, gate_rows = expert_ids.T, gates.T
    bf16, f32 = jnp.bfloat16, jnp.float32

    send, route = pl.pallas_call(
        functools.partial(dispatch_kernel, plan),
        out_shape=(
            jax.ShapeDtypeStruct((experts * plan.send, width), bf16),
            jax.ShapeDtypeStruct((TILE, plan.tok_dev), jnp.int32),
        ),
        name="dispatch",
    )(ids, gate_rows, tokens, out_grad)
    recv = lax.all_to_all(
        send.reshape(experts, plan.send, width),
        "expert",
        split_axis=0,
        concat_axis=0,
        tiled=True,
    )
    recv_other = lax.ppermute(recv, "fsdp", swap)
    block, part = min(256, hidden), min(256, hidden)
    blocks = hidden // block
    anywhere, held = pl.BlockSpec(memory_space=pl.ANY), pl.BlockSpec(memory_space=pltpu.VMEM)
    dma = pltpu.SemaphoreType.DMA

    def matrix(*shape):
        return pltpu.VMEM(shape, bf16)

    pick = pl.pallas_call(
        functools.partial(place_kernel, plan),
        out_shape=jax.ShapeDtypeStruct((plan.tok_dev, experts * plan.back), bf16),
        compiler_params=params(63),
        name="placing",
    )(route)

    firsts = pl.pallas_call(
        stage_kernel,
        in_specs=[anywhere] * 3,
        out_specs=(held,) * 2,
        out_shape=(jax.ShapeDtypeStruct((width, block), bf16),) * 2,
        scratch_shapes=[dma((2,))],
        compiler_params=params(52),
        name="staging",
    )(pick, in_own, out_own)
    back = pl.pallas_call(
        functools.partial(token_kernel, plan, part),
        in_specs=[held] * 3 + [anywhere] * 4,
        out_specs=held,
        out_shape=jax.ShapeDtypeStruct((experts, plan.back, width), bf16),
        scratch_shapes=[
            matrix(slots, width),
            matrix(slots, width),
            pltpu.VMEM((slots, width), f32),
            matrix(2 * blocks, width, block),
            matrix(2 * blocks, width, block),
            dma((2, 2 * blocks)),
        ],
        cost_estimate=pl.CostEstimate(
            flops=12 * slots * width * hidden,
            transcendentals=2 * slots * hidden,
            bytes_accessed=8 * width * hidden,
        ),
        compiler_params=params(52),
        name="token_grad",
    )(recv, *firsts, in_own, out_own, in_other, out_other)
    returned = lax.all_to_all(back, "expert", split_axis=0, concat_axis=0, tiled=True)

    grad_in, grad_out = pl.pallas_call(
        functools.partial(weight_kernel, plan, part),
        in_specs=[held] * 4 + [anywhere] * 2,
        out_specs=(anywhere, anywhere),
        out_shape=(jax.ShapeDtypeStruct((width, hidden), bf16),) * 2,
        scratch_shapes=[
            matrix(2 * slots, width),
            matrix(2 * slots, width),
            matrix(width, 2 * slots),
            matrix(width, 2 * slots),
            matrix(blocks, width, block),
            matrix(blocks, width, block),
            matrix(blocks, width, block),
            matrix(blocks, width, block),
            dma((2, blocks)),
            dma((2, blocks)),
        ],
        cost_estimate=pl.CostEstimate(
            flops=16 * slots * width * hidden,
            transcendentals=2 * slots * hidden,
            bytes_accessed=8 * width * hidden,
        ),
        compiler_params=params(52),
        name="weight_grad",
    )(recv, recv_other, *firsts, in_own, out_own)

    d_tokens, d_gates = pl.pallas_call(
        functools.partial(combine_kernel, plan),
        out_shape=(
            jax.ShapeDtypeStruct((plan.tok_dev, width), bf16),
            jax.ShapeDtypeStruct((2, plan.tok_dev), f32),
        ),
        compiler_params=params(16),
        name="combine",
    )(route, pick, gate_rows, returned.reshape(experts * plan.back, width))
    return d_tokens, d_gates.T, grad_in[None], grad_out[None]


def slot_ranks(route_ids):
    count = route_ids.shape[1]
    same = route_ids[:, :, None] == route_ids[:, None, :]
    earlier = jnp.arange(count)[None, :] < jnp.arange(count)[:, None]
    return jnp.sum(jnp.logical_and(same, earlier[None]), axis=2)


def fill_slots(owner, rows_x, rows_dy, gate_flat):
    valid = owner >= 0
    safe = jnp.where(valid, owner, 0)
    token_row = safe // 2
    x_buf = jnp.where(valid[:, None], rows_x[token_row], jnp.zeros((), rows_x.dtype))
    dy_buf = jnp.where(valid[:, None], rows_dy[token_row], jnp.zeros((), rows_dy.dtype))
    gate_buf = jnp.where(valid, gate_flat[safe], jnp.zeros((), gate_flat.dtype))
    return (x_buf, dy_buf, gate_buf)


def expert_work(x_rows, dy_rows, gate_rows, in_shard, out_shard):
    pre_act = jnp.dot(x_rows, in_shard, preferred_element_type=jnp.float32)
    grad_act = jnp.dot(dy_rows, out_shard, preferred_element_type=jnp.float32)
    values, slopes = gelu_parts(pre_act)
    scale = gate_rows.astype(jnp.float32)[:, None]
    act_scaled = (scale * values).astype(jnp.bfloat16)
    grad_pre = (scale * grad_act * slopes).astype(jnp.bfloat16)
    grad_out = lax.dot_general(dy_rows, act_scaled, ROW_DIMS, preferred_element_type=jnp.float32)
    grad_in = lax.dot_general(x_rows, grad_pre, ROW_DIMS, preferred_element_type=jnp.float32)
    token_part = lax.dot_general(
        grad_pre, in_shard, LAST_DIMS, preferred_element_type=jnp.float32
    ).astype(jnp.bfloat16)
    gate_part = jnp.sum(grad_act * values, axis=1).astype(jnp.bfloat16)
    return (grad_in, grad_out, token_part, gate_part)


def all_rows(plan, tokens, out_grad, gates, expert_ids, w_in, w_out):
    tok_dev, width, groups = plan.tok_dev, plan.width, plan.groups
    experts, capacity = plan.experts, plan.cap
    group_ids = expert_ids.reshape(groups, 2 * tok_dev)
    group_gates = gates.reshape(groups, 2 * tok_dev)
    group_ranks = slot_ranks(group_ids)
    all_x = lax.all_gather(tokens, "fsdp", axis=0, tiled=True)
    all_dy = lax.all_gather(out_grad, "fsdp", axis=0, tiled=True)
    member = jnp.arange(groups, dtype=jnp.int32)[:, None]
    target = ((group_ids * groups + member) * capacity + group_ranks).reshape(-1)
    owner = (
        jnp.full((experts * groups * capacity,), -1, jnp.int32)
        .at[target]
        .set(jnp.arange(2 * tok_dev * groups, dtype=jnp.int32))
    )
    span = groups * capacity
    total_rows = experts * span

    def exchange(rows):
        rows = rows.reshape((experts, span) + rows.shape[1:])
        rows = lax.all_to_all(rows, "expert", split_axis=0, concat_axis=0, tiled=True)
        return rows.reshape((total_rows,) + rows.shape[2:])

    buffers = fill_slots(owner, all_x, all_dy, group_gates.reshape(-1))
    grad_in, grad_out, token_part, gate_part = expert_work(
        *(exchange(b) for b in buffers), w_in[0], w_out[0]
    )
    token_back, gate_back = exchange(token_part), exchange(gate_part)
    token_pick = token_back[target].astype(jnp.float32).reshape(groups * tok_dev, 2, width)
    gate_terms = gate_back[target].astype(jnp.float32).reshape(groups * tok_dev, 2)

    def spread(terms):
        return lax.psum_scatter(
            terms.astype(jnp.bfloat16), "fsdp", scatter_dimension=0, tiled=True
        )

    return (
        spread(jnp.sum(token_pick, axis=1)).astype(jnp.bfloat16),
        spread(gate_terms).astype(jnp.float32),
        grad_in.astype(jnp.bfloat16)[None],
        grad_out.astype(jnp.bfloat16)[None],
    )


def per_device(tokens, out_grad, gates, expert_ids, w_in, w_out):
    plan = Plan(lax.axis_size("expert"), lax.axis_size("fsdp"), *tokens.shape)
    form = moved_rows if plan.fits() else all_rows
    return form(plan, tokens, out_grad, gates, expert_ids, w_in, w_out)


def solution(mesh):
    rows, both = P(("expert", "fsdp"), None), P("expert", None)
    weights = P("expert", None, "fsdp")
    return jax.shard_map(
        per_device,
        mesh=mesh,
        in_specs=(rows, rows, both, both, weights, weights),
        out_specs=(rows, rows, weights, weights),
        check_vma=False,
    )
```

```python
import functools

import jax
import jax.numpy as jnp
from jax import lax
from jax.experimental import pallas as pl
from jax.experimental.pallas import tpu as pltpu
from jax.sharding import PartitionSpec as P


COEF = 0.7978845608
CUBIC = 0.044715
ROW_DIMS = (((0,), (0,)), ((), ()))
LAST_DIMS = (((1,), (1,)), ((), ()))
LANES = 128
TILE = 8
PACK = 16
MIB = 1 << 20


def gelu_parts(pre_act):
    square = pre_act * pre_act
    half = 0.5 + 0.5 * jnp.tanh(pre_act * (COEF + (COEF * CUBIC) * square))
    values = pre_act * half
    slopes = half + values * ((1.0 - half) * (2.0 * COEF + (6.0 * COEF * CUBIC) * square))
    return values, slopes


def iota(shape, dim):
    return lax.broadcasted_iota(jnp.int32, shape, dim)


def split(value, unit):
    return value >> (unit.bit_length() - 1), value & (unit - 1)


def one_hot(mask):
    return jnp.where(mask, 1.0, 0.0).astype(jnp.bfloat16)


class Plan:
    def __init__(self, experts, groups, tok_dev, width):
        self.experts, self.groups, self.tok_dev, self.width = experts, groups, tok_dev, width
        self.cap = 5 * tok_dev // (2 * experts)
        self.main = self.cap // PACK * PACK
        self.tail = self.cap - self.main
        self.send = 2 * self.cap
        self.back = self.main + TILE
        self.slots = experts * self.cap
        self.heads = experts * self.main

    def fits(self):
        return (
            self.groups == 2
            and self.main == PACK
            and 2 * self.tail == TILE
            and self.cap <= LANES
            and self.tok_dev % LANES == 0
            and self.width % LANES == 0
        )


def dispatch_kernel(plan, ids_ref, gates_ref, x_ref, dy_ref, send_ref, route_ref):
    tokens = plan.tok_dev
    mine = pl.ds(pl.multiple_of(lax.axis_index("fsdp") * tokens, LANES), tokens)
    ids = ids_ref[:, mine]
    gates = gates_ref[:, mine].astype(jnp.float32)
    expert = iota((plan.experts, tokens), 0)
    named = [expert == ids[k : k + 1, :] for k in range(2)]
    earlier = one_hot(iota((tokens, tokens), 0) < iota((tokens, tokens), 1))
    counts = jnp.dot(one_hot(named[0] | named[1]), earlier, preferred_element_type=jnp.float32)
    row = iota((plan.experts * plan.send, tokens), 0)
    x_pick, dy_pick = False, 0.0
    for k in range(2):
        rank = jnp.sum(jnp.where(named[k], counts, 0.0), axis=0, keepdims=True).astype(jnp.int32)
        first = ids[k : k + 1, :] * plan.send + rank
        head = rank < plan.main
        x_pick = x_pick | (row == first + jnp.where(head, 0, plan.main))
        dy_pick = dy_pick + jnp.where(
            row == first + jnp.where(head, plan.main, plan.cap), gates[k : k + 1, :], 0.0
        )
        route_ref[k : k + 1, :] = ids[k : k + 1, :]
        route_ref[2 + k : 3 + k, :] = rank
        route_ref[4 + k : 5 + k, :] = jnp.zeros_like(rank)
        route_ref[6 + k : 7 + k, :] = jnp.zeros_like(rank)
    send = jnp.dot(one_hot(x_pick), x_ref[...], preferred_element_type=jnp.float32)
    send = send + jnp.dot(
        dy_pick.astype(jnp.bfloat16), dy_ref[...], preferred_element_type=jnp.float32
    )
    send_ref[...] = send.astype(jnp.bfloat16)


def unpack(plan, recv_ref, x_all, dy_all, at):
    main, tail, width = plan.main, plan.tail, plan.width
    tails = plan.experts * tail
    heads = pl.ds(at, plan.heads)
    x_all[heads, :] = recv_ref[:, :main, :].reshape(plan.heads, width)
    dy_all[heads, :] = recv_ref[:, main : 2 * main, :].reshape(plan.heads, width)
    mixed = recv_ref[:, 2 * main :, :].reshape(plan.experts * TILE, width)
    place, source = iota((2 * tails, plan.experts * TILE), 0), iota(
        (2 * tails, plan.experts * TILE), 1
    )
    second = jnp.where(place >= tails, 1, 0)
    block, rank = split(place - second * tails, tail)
    pick = one_hot(source == block * TILE + rank + second * tail)
    rows = jnp.dot(pick, mixed, preferred_element_type=jnp.float32).astype(jnp.bfloat16)
    x_all[pl.ds(at + plan.heads, tails), :] = rows[:tails]
    dy_all[pl.ds(at + plan.heads, tails), :] = rows[tails:]


def stage_kernel(_, in_hbm, out_hbm, in_first, out_first, sems):
    columns = slice(0, in_first.shape[1])
    copies = [
        pltpu.make_async_copy(ref.at[:, columns], first, sems.at[m])
        for m, (ref, first) in enumerate(((in_hbm, in_first), (out_hbm, out_first)))
    ]
    for copy in copies:
        copy.start()
    for copy in copies:
        copy.wait()


def column_copies(sources, buffers, sems):
    block = buffers[0].shape[2]
    copies = []
    for pair in sources:
        for at in range(0, pair[0].shape[1], block):
            n = len(copies)
            copies.append(
                [
                    pltpu.make_async_copy(
                        ref.at[:, at : at + block], buffers[m].at[n], sems.at[m, n]
                    )
                    for m, ref in enumerate(pair)
                ]
            )
    return copies


def staged(count, ahead, finish):
    held = ahead(0)
    for n in range(count):
        later = ahead(n + 1) if n + 1 < count else None
        finish(n, *held)
        held = later


def part_of(first, buffer, n, part):
    chunk, at = divmod(n * part, buffer.shape[2])
    return first[:, at : at + part] if chunk == 0 else buffer[chunk, :, at : at + part]


def first_acts(x_all, dy_all, firsts, buffers, copies, part):
    block = buffers[0].shape[2]

    def ahead(n):
        chunk, at = divmod(n * part, block)
        if at == 0 and chunk > 0:
            for copy in copies[chunk]:
                copy.wait()
        return tuple(
            jnp.dot(
                rows[...], part_of(first, mat, n, part), preferred_element_type=jnp.float32
            )
            for rows, first, mat in zip((x_all, dy_all), firsts, buffers)
        )

    return ahead


def token_kernel(
    plan, part, recv_ref, in_first, out_first, in_a, out_a, in_b, out_b, back_hbm, x_all, dy_all, total, in_buf, out_buf, heads, rests, sems, store_sems
):
    buffers, firsts = (in_buf, out_buf), (in_first, out_first)
    copies = column_copies(((in_a, out_a), (in_b, out_b)), buffers, sems)
    for pair in copies[1:]:
        for copy in pair:
            copy.start()
    unpack(plan, recv_ref, x_all, dy_all, 0)
    block = in_buf.shape[2]
    gate_lanes = []

    def finish(n, pre_act, grad_act):
        values, slopes = gelu_parts(pre_act)
        grad_pre = (grad_act * slopes).astype(jnp.bfloat16)
        back = lax.dot_general(
            grad_pre,
            part_of(in_first, in_buf, n, part),
            LAST_DIMS,
            preferred_element_type=jnp.float32,
        )
        total[...] = back if n == 0 else total[...] + back
        product = grad_act * values
        for lane in range(0, part, LANES):
            piece = product[:, lane : lane + LANES]
            gate_lanes[:] = [gate_lanes[0] + piece] if gate_lanes else [piece]

    staged(len(copies) * block // part, first_acts(x_all, dy_all, firsts, buffers, copies, part), finish)

    main, tail, width = plan.main, plan.tail, plan.width
    tails = plan.experts * tail
    stores = [
        pltpu.make_async_copy(heads, back_hbm.at[:, :main, :], store_sems.at[0]),
        pltpu.make_async_copy(rests, back_hbm.at[:, main:, :], store_sems.at[1]),
    ]
    heads[...] = (
        total[: plan.heads, :].astype(jnp.bfloat16).reshape(plan.experts, main, width)
    )
    stores[0].start()
    gate = jnp.sum(gate_lanes[0], axis=1, keepdims=True)

    def place_of(slot):
        source, rank = split(slot, main)
        block, over = split(slot - plan.heads, tail)
        late = slot >= plan.heads
        return jnp.where(late, block, source), jnp.where(late, main + over, rank)

    _, rank = place_of(iota((plan.slots, LANES), 0))
    gate_rows = jnp.where(iota((plan.slots, LANES), 1) == rank, gate, 0.0).astype(jnp.bfloat16)
    place = iota((plan.experts * TILE, plan.slots), 0)
    source, _ = place_of(iota((plan.experts * TILE, plan.slots), 1))
    gates = jnp.dot(
        one_hot(place == source * TILE + tail), gate_rows, preferred_element_type=jnp.float32
    )
    place = iota((plan.experts * TILE, tails), 0)
    block, over = split(iota((plan.experts * TILE, tails), 1), tail)
    rest = jnp.dot(
        one_hot(place == block * TILE + over),
        total[plan.heads :, :].astype(jnp.bfloat16),
        preferred_element_type=jnp.float32,
    )
    rest = jnp.concatenate([rest[:, :LANES] + gates, rest[:, LANES:]], axis=1)
    rests[...] = rest.astype(jnp.bfloat16).reshape(plan.experts, TILE, width)
    stores[1].start()
    for store in stores:
        store.wait()


def weight_kernel(
    plan,
    part,
    own_ref,
    other_ref,
    in_first,
    out_first,
    in_ref,
    out_ref,
    grad_in_ref,
    grad_out_ref,
    x_all,
    dy_all,
    x_turned,
    dy_turned,
    in_buf,
    out_buf,
    in_grads,
    out_grads,
    sems,
    done,
):
    buffers, firsts = (in_buf, out_buf), (in_first, out_first)
    copies = column_copies(((in_ref, out_ref),), buffers, sems)
    for pair in copies[1:]:
        for copy in pair:
            copy.start()
    unpack(plan, own_ref, x_all, dy_all, 0)
    unpack(plan, other_ref, x_all, dy_all, plan.slots)
    x_turned[...] = x_all[...].T
    dy_turned[...] = dy_all[...].T
    block = in_buf.shape[2]
    stores = []

    def finish(n, pre_act, grad_act):
        chunk, at = divmod(n * part, block)
        values, slopes = gelu_parts(pre_act)
        grad_pre = (grad_act * slopes).astype(jnp.bfloat16)
        for rows, acts, held in (
            (x_turned, grad_pre, in_grads),
            (dy_turned, values.astype(jnp.bfloat16), out_grads),
        ):
            held[chunk, :, at : at + part] = jnp.dot(
                rows[...], acts, preferred_element_type=jnp.float32
            ).astype(jnp.bfloat16)
        if at + part == block:
            columns = slice(chunk * block, (chunk + 1) * block)
            for m, (held, ref) in enumerate(((in_grads, grad_in_ref), (out_grads, grad_out_ref))):
                stores.append(
                    pltpu.make_async_copy(held.at[chunk], ref.at[:, columns], done.at[m, chunk])
                )
                stores[-1].start()

    staged(len(copies) * block // part, first_acts(x_all, dy_all, firsts, buffers, copies, part), finish)
    for store in stores:
        store.wait()


def place_kernel(plan, route_ref, pick_ref):
    row = iota((plan.experts * plan.back, plan.tok_dev), 0)
    pick = False
    for k in range(2):
        pick = pick | (row == route_ref[k : k + 1, :] * plan.back + route_ref[2 + k : 3 + k, :])
    pick_ref[...] = jnp.where(pick, 1.0, 0.0).T.astype(jnp.bfloat16)


def combine_kernel(plan, route_ref, pick_ref, gates_ref, back_ref, token_ref, gate_ref):
    tokens, rows = plan.tok_dev, plan.experts * plan.back
    mine = pl.ds(pl.multiple_of(lax.axis_index("fsdp") * tokens, LANES), tokens)
    gates = gates_ref[:, mine].astype(jnp.float32)
    back = back_ref[...]
    token_ref[...] = jnp.dot(
        pick_ref[...], back, preferred_element_type=jnp.float32
    ).astype(jnp.bfloat16)
    gate_row = iota((plan.experts, rows), 0) * plan.back + plan.cap
    gate_rows = jnp.dot(
        one_hot(iota((plan.experts, rows), 1) == gate_row),
        back[:, :LANES],
        preferred_element_type=jnp.float32,
    ).astype(jnp.bfloat16)
    for k in range(2):
        named = one_hot(iota((plan.experts, tokens), 0) == route_ref[k : k + 1, :])
        slots = lax.dot_general(gate_rows, named, ROW_DIMS, preferred_element_type=jnp.float32)
        here = iota((LANES, tokens), 0) == route_ref[2 + k : 3 + k, :]
        total = jnp.sum(jnp.where(here, slots, 0.0), axis=0, keepdims=True)
        gate_ref[k : k + 1, :] = total / gates[k : k + 1, :]


def params(mib):
    return pltpu.CompilerParams(vmem_limit_bytes=mib * MIB)


def moved_rows(plan, tokens, out_grad, gates, expert_ids, w_in, w_out):
    experts, width, slots = plan.experts, plan.width, plan.slots
    in_own, out_own = w_in[0], w_out[0]
    hidden = in_own.shape[1]
    swap = [(0, 1), (1, 0)]
    in_other = lax.ppermute(in_own, "fsdp", swap)
    out_other = lax.ppermute(out_own, "fsdp", swap)
    ids, gate_rows = expert_ids.T, gates.T
    bf16, f32 = jnp.bfloat16, jnp.float32

    send, route = pl.pallas_call(
        functools.partial(dispatch_kernel, plan),
        out_shape=(
            jax.ShapeDtypeStruct((experts * plan.send, width), bf16),
            jax.ShapeDtypeStruct((TILE, plan.tok_dev), jnp.int32),
        ),
        name="dispatch",
    )(ids, gate_rows, tokens, out_grad)
    recv = lax.all_to_all(
        send.reshape(experts, plan.send, width),
        "expert",
        split_axis=0,
        concat_axis=0,
        tiled=True,
    )
    recv_other = lax.ppermute(recv, "fsdp", swap)
    block, part = min(256, hidden), min(256, hidden)
    blocks = hidden // block
    anywhere, held = pl.BlockSpec(memory_space=pl.ANY), pl.BlockSpec(memory_space=pltpu.VMEM)
    dma = pltpu.SemaphoreType.DMA

    def matrix(*shape):
        return pltpu.VMEM(shape, bf16)

    pick = pl.pallas_call(
        functools.partial(place_kernel, plan),
        out_shape=jax.ShapeDtypeStruct((plan.tok_dev, experts * plan.back), bf16),
        compiler_params=params(63),
        name="placing",
    )(route)

    firsts = pl.pallas_call(
        stage_kernel,
        in_specs=[anywhere] * 3,
        out_specs=(held,) * 2,
        out_shape=(jax.ShapeDtypeStruct((width, block), bf16),) * 2,
        scratch_shapes=[dma((2,))],
        compiler_params=params(52),
        name="staging",
    )(pick, in_own, out_own)
    back = pl.pallas_call(
        functools.partial(token_kernel, plan, part),
        in_specs=[held] * 3 + [anywhere] * 4,
        out_specs=anywhere,
        out_shape=jax.ShapeDtypeStruct((experts, plan.back, width), bf16),
        scratch_shapes=[
            matrix(slots, width),
            matrix(slots, width),
            pltpu.VMEM((slots, width), f32),
            matrix(2 * blocks, width, block),
            matrix(2 * blocks, width, block),
            matrix(experts, plan.main, width),
            matrix(experts, TILE, width),
            dma((2, 2 * blocks)),
            dma((2,)),
        ],
        cost_estimate=pl.CostEstimate(
            flops=12 * slots * width * hidden,
            transcendentals=2 * slots * hidden,
            bytes_accessed=8 * width * hidden,
        ),
        compiler_params=params(52),
        name="token_grad",
    )(recv, *firsts, in_own, out_own, in_other, out_other)
    returned = lax.all_to_all(back, "expert", split_axis=0, concat_axis=0, tiled=True)

    grad_in, grad_out = pl.pallas_call(
        functools.partial(weight_kernel, plan, part),
        in_specs=[held] * 4 + [anywhere] * 2,
        out_specs=(anywhere, anywhere),
        out_shape=(jax.ShapeDtypeStruct((width, hidden), bf16),) * 2,
        scratch_shapes=[
            matrix(2 * slots, width),
            matrix(2 * slots, width),
            matrix(width, 2 * slots),
            matrix(width, 2 * slots),
            matrix(blocks, width, block),
            matrix(blocks, width, block),
            matrix(blocks, width, block),
            matrix(blocks, width, block),
            dma((2, blocks)),
            dma((2, blocks)),
        ],
        cost_estimate=pl.CostEstimate(
            flops=16 * slots * width * hidden,
            transcendentals=2 * slots * hidden,
            bytes_accessed=8 * width * hidden,
        ),
        compiler_params=params(52),
        name="weight_grad",
    )(recv, recv_other, *firsts, in_own, out_own)

    d_tokens, d_gates = pl.pallas_call(
        functools.partial(combine_kernel, plan),
        out_shape=(
            jax.ShapeDtypeStruct((plan.tok_dev, width), bf16),
            jax.ShapeDtypeStruct((2, plan.tok_dev), f32),
        ),
        compiler_params=params(16),
        name="combine",
    )(route, pick, gate_rows, returned.reshape(experts * plan.back, width))
    return d_tokens, d_gates.T, grad_in[None], grad_out[None]


def slot_ranks(route_ids):
    count = route_ids.shape[1]
    same = route_ids[:, :, None] == route_ids[:, None, :]
    earlier = jnp.arange(count)[None, :] < jnp.arange(count)[:, None]
    return jnp.sum(jnp.logical_and(same, earlier[None]), axis=2)


def fill_slots(owner, rows_x, rows_dy, gate_flat):
    valid = owner >= 0
    safe = jnp.where(valid, owner, 0)
    token_row = safe // 2
    x_buf = jnp.where(valid[:, None], rows_x[token_row], jnp.zeros((), rows_x.dtype))
    dy_buf = jnp.where(valid[:, None], rows_dy[token_row], jnp.zeros((), rows_dy.dtype))
    gate_buf = jnp.where(valid, gate_flat[safe], jnp.zeros((), gate_flat.dtype))
    return (x_buf, dy_buf, gate_buf)


def expert_work(x_rows, dy_rows, gate_rows, in_shard, out_shard):
    pre_act = jnp.dot(x_rows, in_shard, preferred_element_type=jnp.float32)
    grad_act = jnp.dot(dy_rows, out_shard, preferred_element_type=jnp.float32)
    values, slopes = gelu_parts(pre_act)
    scale = gate_rows.astype(jnp.float32)[:, None]
    act_scaled = (scale * values).astype(jnp.bfloat16)
    grad_pre = (scale * grad_act * slopes).astype(jnp.bfloat16)
    grad_out = lax.dot_general(dy_rows, act_scaled, ROW_DIMS, preferred_element_type=jnp.float32)
    grad_in = lax.dot_general(x_rows, grad_pre, ROW_DIMS, preferred_element_type=jnp.float32)
    token_part = lax.dot_general(
        grad_pre, in_shard, LAST_DIMS, preferred_element_type=jnp.float32
    ).astype(jnp.bfloat16)
    gate_part = jnp.sum(grad_act * values, axis=1).astype(jnp.bfloat16)
    return (grad_in, grad_out, token_part, gate_part)


def all_rows(plan, tokens, out_grad, gates, expert_ids, w_in, w_out):
    tok_dev, width, groups = plan.tok_dev, plan.width, plan.groups
    experts, capacity = plan.experts, plan.cap
    group_ids = expert_ids.reshape(groups, 2 * tok_dev)
    group_gates = gates.reshape(groups, 2 * tok_dev)
    group_ranks = slot_ranks(group_ids)
    all_x = lax.all_gather(tokens, "fsdp", axis=0, tiled=True)
    all_dy = lax.all_gather(out_grad, "fsdp", axis=0, tiled=True)
    member = jnp.arange(groups, dtype=jnp.int32)[:, None]
    target = ((group_ids * groups + member) * capacity + group_ranks).reshape(-1)
    owner = (
        jnp.full((experts * groups * capacity,), -1, jnp.int32)
        .at[target]
        .set(jnp.arange(2 * tok_dev * groups, dtype=jnp.int32))
    )
    span = groups * capacity
    total_rows = experts * span

    def exchange(rows):
        rows = rows.reshape((experts, span) + rows.shape[1:])
        rows = lax.all_to_all(rows, "expert", split_axis=0, concat_axis=0, tiled=True)
        return rows.reshape((total_rows,) + rows.shape[2:])

    buffers = fill_slots(owner, all_x, all_dy, group_gates.reshape(-1))
    grad_in, grad_out, token_part, gate_part = expert_work(
        *(exchange(b) for b in buffers), w_in[0], w_out[0]
    )
    token_back, gate_back = exchange(token_part), exchange(gate_part)
    token_pick = token_back[target].astype(jnp.float32).reshape(groups * tok_dev, 2, width)
    gate_terms = gate_back[target].astype(jnp.float32).reshape(groups * tok_dev, 2)

    def spread(terms):
        return lax.psum_scatter(
            terms.astype(jnp.bfloat16), "fsdp", scatter_dimension=0, tiled=True
        )

    return (
        spread(jnp.sum(token_pick, axis=1)).astype(jnp.bfloat16),
        spread(gate_terms).astype(jnp.float32),
        grad_in.astype(jnp.bfloat16)[None],
        grad_out.astype(jnp.bfloat16)[None],
    )


def per_device(tokens, out_grad, gates, expert_ids, w_in, w_out):
    plan = Plan(lax.axis_size("expert"), lax.axis_size("fsdp"), *tokens.shape)
    form = moved_rows if plan.fits() else all_rows
    return form(plan, tokens, out_grad, gates, expert_ids, w_in, w_out)


def solution(mesh):
    rows, both = P(("expert", "fsdp"), None), P("expert", None)
    weights = P("expert", None, "fsdp")
    return jax.shard_map(
        per_device,
        mesh=mesh,
        in_specs=(rows, rows, both, both, weights, weights),
        out_specs=(rows, rows, weights, weights),
        check_vma=False,
    )
```

```python
import functools

import jax
import jax.numpy as jnp
from jax import lax
from jax.experimental import pallas as pl
from jax.experimental.pallas import tpu as pltpu
from jax.sharding import PartitionSpec as P


COEF = 0.7978845608
CUBIC = 0.044715
ROW_DIMS = (((0,), (0,)), ((), ()))
LAST_DIMS = (((1,), (1,)), ((), ()))
LANES = 128
TILE = 8
PACK = 16
MIB = 1 << 20
GROUP = 3


def gelu_parts(pre_act):
    square = pre_act * pre_act
    half = 0.5 + 0.5 * jnp.tanh(pre_act * (COEF + (COEF * CUBIC) * square))
    values = pre_act * half
    slopes = half + values * ((1.0 - half) * (2.0 * COEF + (6.0 * COEF * CUBIC) * square))
    return values, slopes


def iota(shape, dim):
    return lax.broadcasted_iota(jnp.int32, shape, dim)


def split(value, unit):
    return value >> (unit.bit_length() - 1), value & (unit - 1)


def one_hot(mask):
    return jnp.where(mask, 1.0, 0.0).astype(jnp.bfloat16)


class Plan:
    def __init__(self, experts, groups, tok_dev, width):
        self.experts, self.groups, self.tok_dev, self.width = experts, groups, tok_dev, width
        self.cap = 5 * tok_dev // (2 * experts)
        self.main = self.cap // PACK * PACK
        self.tail = self.cap - self.main
        self.send = 2 * self.cap
        self.back = self.main + TILE
        self.slots = experts * self.cap
        self.heads = experts * self.main

    def fits(self):
        return (
            self.groups == 2
            and self.main == PACK
            and 2 * self.tail == TILE
            and self.cap <= LANES
            and self.tok_dev % LANES == 0
            and self.width % LANES == 0
        )


def dispatch_kernel(plan, ids_ref, gates_ref, x_ref, dy_ref, send_ref, route_ref):
    tokens = plan.tok_dev
    mine = pl.ds(pl.multiple_of(lax.axis_index("fsdp") * tokens, LANES), tokens)
    ids = ids_ref[:, mine]
    gates = gates_ref[:, mine].astype(jnp.float32)
    expert = iota((plan.experts, tokens), 0)
    named = [expert == ids[k : k + 1, :] for k in range(2)]
    earlier = one_hot(iota((tokens, tokens), 0) < iota((tokens, tokens), 1))
    counts = jnp.dot(one_hot(named[0] | named[1]), earlier, preferred_element_type=jnp.float32)
    row = iota((plan.experts * plan.send, tokens), 0)
    x_pick, dy_pick = False, 0.0
    for k in range(2):
        rank = jnp.sum(jnp.where(named[k], counts, 0.0), axis=0, keepdims=True).astype(jnp.int32)
        first = ids[k : k + 1, :] * plan.send + rank
        head = rank < plan.main
        x_pick = x_pick | (row == first + jnp.where(head, 0, plan.main))
        dy_pick = dy_pick + jnp.where(
            row == first + jnp.where(head, plan.main, plan.cap), gates[k : k + 1, :], 0.0
        )
        route_ref[k : k + 1, :] = ids[k : k + 1, :]
        route_ref[2 + k : 3 + k, :] = rank
        route_ref[4 + k : 5 + k, :] = jnp.zeros_like(rank)
        route_ref[6 + k : 7 + k, :] = jnp.zeros_like(rank)
    send = jnp.dot(one_hot(x_pick), x_ref[...], preferred_element_type=jnp.float32)
    send = send + jnp.dot(
        dy_pick.astype(jnp.bfloat16), dy_ref[...], preferred_element_type=jnp.float32
    )
    send_ref[...] = send.astype(jnp.bfloat16)


def unpack(plan, recv_ref, x_all, dy_all, at):
    main, tail, width = plan.main, plan.tail, plan.width
    tails = plan.experts * tail
    heads = pl.ds(at, plan.heads)
    x_all[heads, :] = recv_ref[:, :main, :].reshape(plan.heads, width)
    dy_all[heads, :] = recv_ref[:, main : 2 * main, :].reshape(plan.heads, width)
    mixed = recv_ref[:, 2 * main :, :].reshape(plan.experts * TILE, width)
    place, source = iota((2 * tails, plan.experts * TILE), 0), iota(
        (2 * tails, plan.experts * TILE), 1
    )
    second = jnp.where(place >= tails, 1, 0)
    block, rank = split(place - second * tails, tail)
    pick = one_hot(source == block * TILE + rank + second * tail)
    rows = jnp.dot(pick, mixed, preferred_element_type=jnp.float32).astype(jnp.bfloat16)
    x_all[pl.ds(at + plan.heads, tails), :] = rows[:tails]
    dy_all[pl.ds(at + plan.heads, tails), :] = rows[tails:]


def stage_kernel(_, in_hbm, out_hbm, in_first, out_first, sems):
    columns = slice(0, in_first.shape[1])
    copies = [
        pltpu.make_async_copy(ref.at[:, columns], first, sems.at[m])
        for m, (ref, first) in enumerate(((in_hbm, in_first), (out_hbm, out_first)))
    ]
    for copy in copies:
        copy.start()
    for copy in copies:
        copy.wait()


def column_copies(sources, buffers, sems):
    block = buffers[0].shape[2]
    copies = []
    for pair in sources:
        for at in range(0, pair[0].shape[1], block):
            n = len(copies)
            copies.append(
                [
                    pltpu.make_async_copy(
                        ref.at[:, at : at + block], buffers[m].at[n], sems.at[m, n]
                    )
                    for m, ref in enumerate(pair)
                ]
            )
    return copies


def staged(count, ahead, finish):
    held = ahead(0)
    for n in range(count):
        later = ahead(n + 1) if n + 1 < count else None
        finish(n, *held)
        held = later


def part_of(first, buffer, n, part):
    chunk, at = divmod(n * part, buffer.shape[2])
    return first[:, at : at + part] if chunk == 0 else buffer[chunk, :, at : at + part]


def first_acts(x_all, dy_all, firsts, buffers, copies, part, group=1):
    block = buffers[0].shape[2]

    def ahead(n):
        chunk, at = divmod(n * part, block)
        if at == 0 and chunk % group == 1 % group:
            for pair in copies[max(chunk, 1) : chunk + group]:
                for copy in pair:
                    copy.wait()
        return tuple(
            jnp.dot(
                rows[...], part_of(first, mat, n, part), preferred_element_type=jnp.float32
            )
            for rows, first, mat in zip((x_all, dy_all), firsts, buffers)
        )

    return ahead


def token_kernel(
    plan, part, recv_ref, in_first, out_first, in_a, out_a, in_b, out_b, back_hbm, x_all, dy_all, total, in_buf, out_buf, heads, rests, sems, store_sems
):
    buffers, firsts = (in_buf, out_buf), (in_first, out_first)
    copies = column_copies(((in_a, out_a), (in_b, out_b)), buffers, sems)
    for pair in copies[1:]:
        for copy in pair:
            copy.start()
    unpack(plan, recv_ref, x_all, dy_all, 0)
    block = in_buf.shape[2]
    gate_lanes = []

    def finish(n, pre_act, grad_act):
        values, slopes = gelu_parts(pre_act)
        grad_pre = (grad_act * slopes).astype(jnp.bfloat16)
        back = lax.dot_general(
            grad_pre,
            part_of(in_first, in_buf, n, part),
            LAST_DIMS,
            preferred_element_type=jnp.float32,
        )
        total[...] = back if n == 0 else total[...] + back
        product = grad_act * values
        for lane in range(0, part, LANES):
            piece = product[:, lane : lane + LANES]
            gate_lanes[:] = [gate_lanes[0] + piece] if gate_lanes else [piece]

    staged(len(copies) * block // part, first_acts(x_all, dy_all, firsts, buffers, copies, part, GROUP), finish)

    main, tail, width = plan.main, plan.tail, plan.width
    tails = plan.experts * tail
    stores = [
        pltpu.make_async_copy(heads, back_hbm.at[:, :main, :], store_sems.at[0]),
        pltpu.make_async_copy(rests, back_hbm.at[:, main:, :], store_sems.at[1]),
    ]
    heads[...] = (
        total[: plan.heads, :].astype(jnp.bfloat16).reshape(plan.experts, main, width)
    )
    stores[0].start()
    gate = jnp.sum(gate_lanes[0], axis=1, keepdims=True)

    def place_of(slot):
        source, rank = split(slot, main)
        block, over = split(slot - plan.heads, tail)
        late = slot >= plan.heads
        return jnp.where(late, block, source), jnp.where(late, main + over, rank)

    _, rank = place_of(iota((plan.slots, LANES), 0))
    gate_rows = jnp.where(iota((plan.slots, LANES), 1) == rank, gate, 0.0).astype(jnp.bfloat16)
    place = iota((plan.experts * TILE, plan.slots), 0)
    source, _ = place_of(iota((plan.experts * TILE, plan.slots), 1))
    gates = jnp.dot(
        one_hot(place == source * TILE + tail), gate_rows, preferred_element_type=jnp.float32
    )
    place = iota((plan.experts * TILE, tails), 0)
    block, over = split(iota((plan.experts * TILE, tails), 1), tail)
    rest = jnp.dot(
        one_hot(place == block * TILE + over),
        total[plan.heads :, :].astype(jnp.bfloat16),
        preferred_element_type=jnp.float32,
    )
    rest = jnp.concatenate([rest[:, :LANES] + gates, rest[:, LANES:]], axis=1)
    rests[...] = rest.astype(jnp.bfloat16).reshape(plan.experts, TILE, width)
    stores[1].start()
    for store in stores:
        store.wait()


def weight_kernel(
    plan,
    part,
    own_ref,
    other_ref,
    in_first,
    out_first,
    in_ref,
    out_ref,
    grad_in_ref,
    grad_out_ref,
    x_all,
    dy_all,
    x_turned,
    dy_turned,
    in_buf,
    out_buf,
    in_grads,
    out_grads,
    sems,
    done,
):
    buffers, firsts = (in_buf, out_buf), (in_first, out_first)
    copies = column_copies(((in_ref, out_ref),), buffers, sems)
    for pair in copies[1:]:
        for copy in pair:
            copy.start()
    unpack(plan, own_ref, x_all, dy_all, 0)
    unpack(plan, other_ref, x_all, dy_all, plan.slots)
    x_turned[...] = x_all[...].T
    dy_turned[...] = dy_all[...].T
    block = in_buf.shape[2]
    stores = []

    def finish(n, pre_act, grad_act):
        chunk, at = divmod(n * part, block)
        values, slopes = gelu_parts(pre_act)
        grad_pre = (grad_act * slopes).astype(jnp.bfloat16)
        for rows, acts, held in (
            (x_turned, grad_pre, in_grads),
            (dy_turned, values.astype(jnp.bfloat16), out_grads),
        ):
            held[chunk, :, at : at + part] = jnp.dot(
                rows[...], acts, preferred_element_type=jnp.float32
            ).astype(jnp.bfloat16)
        if at + part == block:
            columns = slice(chunk * block, (chunk + 1) * block)
            for m, (held, ref) in enumerate(((in_grads, grad_in_ref), (out_grads, grad_out_ref))):
                stores.append(
                    pltpu.make_async_copy(held.at[chunk], ref.at[:, columns], done.at[m, chunk])
                )
                stores[-1].start()

    staged(len(copies) * block // part, first_acts(x_all, dy_all, firsts, buffers, copies, part), finish)
    for store in stores:
        store.wait()


def place_kernel(plan, route_ref, pick_ref):
    row = iota((plan.experts * plan.back, plan.tok_dev), 0)
    pick = False
    for k in range(2):
        pick = pick | (row == route_ref[k : k + 1, :] * plan.back + route_ref[2 + k : 3 + k, :])
    pick_ref[...] = jnp.where(pick, 1.0, 0.0).T.astype(jnp.bfloat16)


def combine_kernel(plan, route_ref, pick_ref, gates_ref, back_ref, token_ref, gate_ref):
    tokens, rows = plan.tok_dev, plan.experts * plan.back
    mine = pl.ds(pl.multiple_of(lax.axis_index("fsdp") * tokens, LANES), tokens)
    gates = gates_ref[:, mine].astype(jnp.float32)
    back = back_ref[...]
    token_ref[...] = jnp.dot(
        pick_ref[...], back, preferred_element_type=jnp.float32
    ).astype(jnp.bfloat16)
    gate_row = iota((plan.experts, rows), 0) * plan.back + plan.cap
    gate_rows = jnp.dot(
        one_hot(iota((plan.experts, rows), 1) == gate_row),
        back[:, :LANES],
        preferred_element_type=jnp.float32,
    ).astype(jnp.bfloat16)
    for k in range(2):
        named = one_hot(iota((plan.experts, tokens), 0) == route_ref[k : k + 1, :])
        slots = lax.dot_general(gate_rows, named, ROW_DIMS, preferred_element_type=jnp.float32)
        here = iota((LANES, tokens), 0) == route_ref[2 + k : 3 + k, :]
        total = jnp.sum(jnp.where(here, slots, 0.0), axis=0, keepdims=True)
        gate_ref[k : k + 1, :] = total / gates[k : k + 1, :]


def params(mib):
    return pltpu.CompilerParams(vmem_limit_bytes=mib * MIB)


def moved_rows(plan, tokens, out_grad, gates, expert_ids, w_in, w_out):
    experts, width, slots = plan.experts, plan.width, plan.slots
    in_own, out_own = w_in[0], w_out[0]
    hidden = in_own.shape[1]
    swap = [(0, 1), (1, 0)]
    in_other = lax.ppermute(in_own, "fsdp", swap)
    out_other = lax.ppermute(out_own, "fsdp", swap)
    ids, gate_rows = expert_ids.T, gates.T
    bf16, f32 = jnp.bfloat16, jnp.float32

    send, route = pl.pallas_call(
        functools.partial(dispatch_kernel, plan),
        out_shape=(
            jax.ShapeDtypeStruct((experts * plan.send, width), bf16),
            jax.ShapeDtypeStruct((TILE, plan.tok_dev), jnp.int32),
        ),
        name="dispatch",
    )(ids, gate_rows, tokens, out_grad)
    recv = lax.all_to_all(
        send.reshape(experts, plan.send, width),
        "expert",
        split_axis=0,
        concat_axis=0,
        tiled=True,
    )
    recv_other = lax.ppermute(recv, "fsdp", swap)
    block, part = min(256, hidden), min(256, hidden)
    blocks = hidden // block
    anywhere, held = pl.BlockSpec(memory_space=pl.ANY), pl.BlockSpec(memory_space=pltpu.VMEM)
    dma = pltpu.SemaphoreType.DMA

    def matrix(*shape):
        return pltpu.VMEM(shape, bf16)

    pick = pl.pallas_call(
        functools.partial(place_kernel, plan),
        out_shape=jax.ShapeDtypeStruct((plan.tok_dev, experts * plan.back), bf16),
        compiler_params=params(63),
        name="placing",
    )(route)

    firsts = pl.pallas_call(
        stage_kernel,
        in_specs=[anywhere] * 3,
        out_specs=(held,) * 2,
        out_shape=(jax.ShapeDtypeStruct((width, block), bf16),) * 2,
        scratch_shapes=[dma((2,))],
        compiler_params=params(52),
        name="staging",
    )(pick, in_own, out_own)
    back = pl.pallas_call(
        functools.partial(token_kernel, plan, part),
        in_specs=[held] * 3 + [anywhere] * 4,
        out_specs=anywhere,
        out_shape=jax.ShapeDtypeStruct((experts, plan.back, width), bf16),
        scratch_shapes=[
            matrix(slots, width),
            matrix(slots, width),
            pltpu.VMEM((slots, width), f32),
            matrix(2 * blocks, width, block),
            matrix(2 * blocks, width, block),
            matrix(experts, plan.main, width),
            matrix(experts, TILE, width),
            dma((2, 2 * blocks)),
            dma((2,)),
        ],
        cost_estimate=pl.CostEstimate(
            flops=12 * slots * width * hidden,
            transcendentals=2 * slots * hidden,
            bytes_accessed=8 * width * hidden,
        ),
        compiler_params=params(52),
        name="token_grad",
    )(recv, *firsts, in_own, out_own, in_other, out_other)
    returned = lax.all_to_all(back, "expert", split_axis=0, concat_axis=0, tiled=True)

    grad_in, grad_out = pl.pallas_call(
        functools.partial(weight_kernel, plan, part),
        in_specs=[held] * 4 + [anywhere] * 2,
        out_specs=(anywhere, anywhere),
        out_shape=(jax.ShapeDtypeStruct((width, hidden), bf16),) * 2,
        scratch_shapes=[
            matrix(2 * slots, width),
            matrix(2 * slots, width),
            matrix(width, 2 * slots),
            matrix(width, 2 * slots),
            matrix(blocks, width, block),
            matrix(blocks, width, block),
            matrix(blocks, width, block),
            matrix(blocks, width, block),
            dma((2, blocks)),
            dma((2, blocks)),
        ],
        cost_estimate=pl.CostEstimate(
            flops=16 * slots * width * hidden,
            transcendentals=2 * slots * hidden,
            bytes_accessed=8 * width * hidden,
        ),
        compiler_params=params(52),
        name="weight_grad",
    )(recv, recv_other, *firsts, in_own, out_own)

    d_tokens, d_gates = pl.pallas_call(
        functools.partial(combine_kernel, plan),
        out_shape=(
            jax.ShapeDtypeStruct((plan.tok_dev, width), bf16),
            jax.ShapeDtypeStruct((2, plan.tok_dev), f32),
        ),
        compiler_params=params(16),
        name="combine",
    )(route, pick, gate_rows, returned.reshape(experts * plan.back, width))
    return d_tokens, d_gates.T, grad_in[None], grad_out[None]


def slot_ranks(route_ids):
    count = route_ids.shape[1]
    same = route_ids[:, :, None] == route_ids[:, None, :]
    earlier = jnp.arange(count)[None, :] < jnp.arange(count)[:, None]
    return jnp.sum(jnp.logical_and(same, earlier[None]), axis=2)


def fill_slots(owner, rows_x, rows_dy, gate_flat):
    valid = owner >= 0
    safe = jnp.where(valid, owner, 0)
    token_row = safe // 2
    x_buf = jnp.where(valid[:, None], rows_x[token_row], jnp.zeros((), rows_x.dtype))
    dy_buf = jnp.where(valid[:, None], rows_dy[token_row], jnp.zeros((), rows_dy.dtype))
    gate_buf = jnp.where(valid, gate_flat[safe], jnp.zeros((), gate_flat.dtype))
    return (x_buf, dy_buf, gate_buf)


def expert_work(x_rows, dy_rows, gate_rows, in_shard, out_shard):
    pre_act = jnp.dot(x_rows, in_shard, preferred_element_type=jnp.float32)
    grad_act = jnp.dot(dy_rows, out_shard, preferred_element_type=jnp.float32)
    values, slopes = gelu_parts(pre_act)
    scale = gate_rows.astype(jnp.float32)[:, None]
    act_scaled = (scale * values).astype(jnp.bfloat16)
    grad_pre = (scale * grad_act * slopes).astype(jnp.bfloat16)
    grad_out = lax.dot_general(dy_rows, act_scaled, ROW_DIMS, preferred_element_type=jnp.float32)
    grad_in = lax.dot_general(x_rows, grad_pre, ROW_DIMS, preferred_element_type=jnp.float32)
    token_part = lax.dot_general(
        grad_pre, in_shard, LAST_DIMS, preferred_element_type=jnp.float32
    ).astype(jnp.bfloat16)
    gate_part = jnp.sum(grad_act * values, axis=1).astype(jnp.bfloat16)
    return (grad_in, grad_out, token_part, gate_part)


def all_rows(plan, tokens, out_grad, gates, expert_ids, w_in, w_out):
    tok_dev, width, groups = plan.tok_dev, plan.width, plan.groups
    experts, capacity = plan.experts, plan.cap
    group_ids = expert_ids.reshape(groups, 2 * tok_dev)
    group_gates = gates.reshape(groups, 2 * tok_dev)
    group_ranks = slot_ranks(group_ids)
    all_x = lax.all_gather(tokens, "fsdp", axis=0, tiled=True)
    all_dy = lax.all_gather(out_grad, "fsdp", axis=0, tiled=True)
    member = jnp.arange(groups, dtype=jnp.int32)[:, None]
    target = ((group_ids * groups + member) * capacity + group_ranks).reshape(-1)
    owner = (
        jnp.full((experts * groups * capacity,), -1, jnp.int32)
        .at[target]
        .set(jnp.arange(2 * tok_dev * groups, dtype=jnp.int32))
    )
    span = groups * capacity
    total_rows = experts * span

    def exchange(rows):
        rows = rows.reshape((experts, span) + rows.shape[1:])
        rows = lax.all_to_all(rows, "expert", split_axis=0, concat_axis=0, tiled=True)
        return rows.reshape((total_rows,) + rows.shape[2:])

    buffers = fill_slots(owner, all_x, all_dy, group_gates.reshape(-1))
    grad_in, grad_out, token_part, gate_part = expert_work(
        *(exchange(b) for b in buffers), w_in[0], w_out[0]
    )
    token_back, gate_back = exchange(token_part), exchange(gate_part)
    token_pick = token_back[target].astype(jnp.float32).reshape(groups * tok_dev, 2, width)
    gate_terms = gate_back[target].astype(jnp.float32).reshape(groups * tok_dev, 2)

    def spread(terms):
        return lax.psum_scatter(
            terms.astype(jnp.bfloat16), "fsdp", scatter_dimension=0, tiled=True
        )

    return (
        spread(jnp.sum(token_pick, axis=1)).astype(jnp.bfloat16),
        spread(gate_terms).astype(jnp.float32),
        grad_in.astype(jnp.bfloat16)[None],
        grad_out.astype(jnp.bfloat16)[None],
    )


def per_device(tokens, out_grad, gates, expert_ids, w_in, w_out):
    plan = Plan(lax.axis_size("expert"), lax.axis_size("fsdp"), *tokens.shape)
    form = moved_rows if plan.fits() else all_rows
    return form(plan, tokens, out_grad, gates, expert_ids, w_in, w_out)


def solution(mesh):
    rows, both = P(("expert", "fsdp"), None), P("expert", None)
    weights = P("expert", None, "fsdp")
    return jax.shard_map(
        per_device,
        mesh=mesh,
        in_specs=(rows, rows, both, both, weights, weights),
        out_specs=(rows, rows, weights, weights),
        check_vma=False,
    )
```
